256 devices in a mesh: leaf: 64 (over z, y, core), samp: 4 (over x).
Axes of the slice: x: 4, y: 4, z: 8, core: 2. Of those that a mesh axis runs over, the one named last changes fastest.
Arguments:
- points: bfloat16 [8, 131072], P(None, 'leaf'), may hold values from -6 to 6
- omega: bfloat16 [131072, 512], P('leaf', 'samp'), may hold values from -1.1953125 to 1.1953125
- near_lists: int32 [256, 8], replicated, may hold values from 0 to 255, as said below
- leaf_order: int32 [256], replicated, may hold values from 0 to 255, as said below
- pivots: int32 [256, 128], P('leaf'), may hold values from 0 to 511, as said below
Outputs:
- interpolation: bfloat16 [131072, 128], P('leaf')
- parent_rows: float32 [32768, 512], P('leaf', 'samp')
The draws below stay inside these ranges and needn't reach their ends.
Inputs may be any that keep to these rules, and one draw needn't show every extreme that they name: `near_lists`: entries of a row are distinct initial leaf numbers. Mapped through leaf_order, the rows of one aligned block of 4 tree-order leaves name at most 2 distinct leaves of any one aligned block of 4 tree-order leaves, and exactly 2 for some such block; a leaf may be named in several rows. `leaf_order`: A permutation. `pivots`: entries of a row are distinct.
All inputs are finite; a program needn't handle non-finite values.
Results may differ from the reference program's by a relative error of at most 0.013.
Values may be sent and summed in bfloat16 or wider, within the bound.
No kernel may reach another device: no remote copies, remote signals or barrier semaphores. Data moves between devices by JAX's collectives and lax.ppermute only.
A program may use at most 128 MiB of HBM per device.

```python
import jax
import jax.numpy as jnp
from jax import lax

DIMS = 8
LEAF_PTS = 512
NEAR = 8
SKEL = 128
SAMPLES = 512
SLOTS = 2
LEAF_DEV = 4
LEAVES = 256
POINTS = 131072
REACH = 3


def leaf_tables(key):
    base_key = jax.random.fold_in(key, 11)
    split_keys = jax.random.split(base_key, 2)
    position = jax.random.permutation(split_keys[0], LEAVES).astype(jnp.int32)
    inverse = jnp.zeros((LEAVES,), jnp.int32).at[position].set(jnp.arange(LEAVES, dtype=jnp.int32))
    nodes = LEAVES // LEAF_DEV
    window = 2 * REACH + 1
    pool = window * SLOTS
    stride = max(1, (pool - NEAR + LEAF_DEV - 2) // (LEAF_DEV - 1))
    offsets = jnp.concatenate([jnp.arange(window - 1, dtype=jnp.int32) - REACH, jnp.array([nodes // 2], dtype=jnp.int32)])

    def one_node(node):
        sub_keys = jax.random.split(jax.random.fold_in(split_keys[1], node), 2)
        pool_ids = jnp.arange(pool, dtype=jnp.int32)

        def one_source(offset):
            return jax.random.permutation(jax.random.fold_in(sub_keys[0], offset), LEAF_DEV).astype(jnp.int32)
        leaf_picks = jax.vmap(one_source)(jnp.arange(window, dtype=jnp.int32))
        chosen = leaf_picks[pool_ids // SLOTS, pool_ids % SLOTS]
        source_nodes = (node + offsets[pool_ids // SLOTS]) % nodes
        pool_leaves = source_nodes * LEAF_DEV + chosen
        shuffle = jax.random.permutation(sub_keys[1], pool).astype(jnp.int32)
        member = jnp.arange(LEAF_DEV, dtype=jnp.int32)[:, None]
        entry = jnp.arange(NEAR, dtype=jnp.int32)[None, :]
        index = (member * stride + entry) % pool
        return pool_leaves[shuffle[index]]
    tree_lists = jax.vmap(one_node)(jnp.arange(nodes, dtype=jnp.int32)).reshape(LEAVES, NEAR)
    return (position, inverse[tree_lists])


def draw_leaf_order(key, part):
    return leaf_tables(key)[0]


def draw_near_lists(key, part):
    return leaf_tables(key)[1]


def draw_pivots(key, part):
    base_key = jax.random.fold_in(key, 23)

    def one_leaf(leaf_id):
        return jax.random.permutation(jax.random.fold_in(base_key, leaf_id), LEAF_PTS)[:SKEL].astype(jnp.int32)
    return jax.vmap(one_leaf)(jnp.arange(LEAVES, dtype=jnp.int32))


def block_scale(key, shape, shards, least, largest):
    def one(dim, shards_of):
        draws = jax.random.uniform(jax.random.fold_in(jax.random.fold_in(key, 6), dim), (shards_of,), jnp.float32, least / len(shards), largest / len(shards))
        return jnp.repeat(jnp.exp(draws), shape[dim] // shards_of).reshape((-1,) + (1,) * (len(shape) - dim - 1))

    gain = one(*shards[0])
    for cut in shards[1:]:
        gain = gain * one(*cut)
    return gain


def centred(key, dims, deviation, bound, shards=(), kind=jnp.bfloat16):
    factor_of = block_scale(key, dims, shards, -0.22, 0.18) if shards else 1.0
    entries = jax.random.normal(key, dims, jnp.float32) * deviation * factor_of
    return jnp.minimum(jnp.maximum(entries, -bound), bound).astype(kind)


def setup_inputs(seed: int = 0) -> dict:
    streams_of = jax.random.split(jax.random.key(seed), 6)
    return {
        "points": centred(streams_of[0], (DIMS, POINTS), 1.0, 6.0, ((1, 64),)),
        "omega": centred(streams_of[1], (POINTS, SAMPLES), 0.2, 1.1953125, ((0, 64), (1, 4))),
        "near_lists": draw_near_lists(jax.random.fold_in(streams_of[5], 71), 0),
        "leaf_order": draw_leaf_order(jax.random.fold_in(streams_of[5], 71), 0),
        "pivots": draw_pivots(jax.random.fold_in(streams_of[5], 71), 0),
    }


kernel_rate = 0.25
ridge_share = 0.1

def kernel_tile(left_points, right_points):
    left_f = left_points.astype(jnp.float32)
    right_f = right_points.astype(jnp.float32)
    inner = jnp.dot(left_points.T.astype(jnp.float32), right_points.astype(jnp.float32), preferred_element_type=jnp.float32)
    distance = jnp.sum(left_f * left_f, 0)[:, None] + jnp.sum(right_f * right_f, 0)[None, :] - 2.0 * inner
    return jnp.exp(-kernel_rate * distance).astype(jnp.bfloat16)

def factorize(gram_sum):
    trace_value = jnp.trace(gram_sum, axis1=1, axis2=2)
    shift_value = ridge_share * trace_value / SKEL
    eye_matrix = jnp.eye(gram_sum.shape[1], dtype=jnp.float32)
    return jnp.linalg.cholesky(gram_sum + shift_value[:, None, None] * eye_matrix[None])

def solve_rows(factor, row_block):
    half_way = lax.linalg.triangular_solve(factor, row_block, left_side=False, lower=True, transpose_a=True)
    return lax.linalg.triangular_solve(factor, half_way, left_side=False, lower=True, transpose_a=False)

def reference(points, omega, near_lists, leaf_order, pivots):
    tree_lists = jnp.take(leaf_order, near_lists, axis=0)
    leaf_points = points.reshape(DIMS, LEAVES, LEAF_PTS)
    leaf_samples = omega.reshape(LEAVES, LEAF_PTS, SAMPLES)

    def near_sample(leaf_id):
        neighbours = tree_lists[leaf_id]
        far_points = jnp.take(leaf_points, neighbours, axis=1).reshape(DIMS, NEAR * LEAF_PTS)
        far_samples = jnp.take(leaf_samples, neighbours, axis=0).reshape(NEAR * LEAF_PTS, SAMPLES)
        own_points = jnp.take(leaf_points, leaf_id, axis=1)
        return jnp.dot(kernel_tile(own_points, far_points).astype(jnp.float32), far_samples.astype(jnp.float32), preferred_element_type=jnp.float32)
    sampled = lax.map(near_sample, jnp.arange(LEAVES, dtype=jnp.int32))
    skel_rows = jnp.take_along_axis(sampled, pivots[:, :, None], axis=1)
    gram_sum = jnp.einsum('ask,atk->ast', skel_rows, skel_rows, precision=lax.Precision.HIGHEST)
    cross_sum = jnp.einsum('apk,atk->apt', sampled, skel_rows, precision=lax.Precision.HIGHEST)
    interpolation = solve_rows(factorize(gram_sum), cross_sum).astype(jnp.bfloat16)
    projected = jnp.einsum('apt,apk->atk', interpolation.astype(jnp.float32), leaf_samples.astype(jnp.float32), precision=lax.Precision.HIGHEST).astype(jnp.bfloat16)
    skeleton = jnp.take_along_axis(leaf_points, pivots[None, :, :], axis=2)
    node_count = LEAVES // LEAF_DEV
    node_points = skeleton.reshape(DIMS, node_count, LEAF_DEV * SKEL)
    node_projected = projected.reshape(node_count, LEAF_DEV * SKEL, SAMPLES)
    node_rows = skel_rows.reshape(node_count, LEAF_DEV * SKEL, SAMPLES)

    def parent(node_id):
        sibling = jnp.bitwise_xor(node_id, 1)
        coupling = kernel_tile(jnp.take(node_points, node_id, axis=1), jnp.take(node_points, sibling, axis=1))
        return node_rows[node_id] - jnp.dot(coupling.astype(jnp.float32), node_projected[sibling].astype(jnp.float32), preferred_element_type=jnp.float32)
    parent_rows = lax.map(parent, jnp.arange(node_count, dtype=jnp.int32)).reshape(LEAVES * SKEL, SAMPLES)
    return (interpolation.reshape(LEAVES * LEAF_PTS, SKEL), parent_rows)
```

```python
import functools

import jax
import jax.numpy as jnp
from jax import lax
from jax.experimental import pallas as pl
from jax.experimental.pallas import tpu as pltpu
from jax.sharding import PartitionSpec as P

DIMS = 8
LEAF_PTS = 512
NEAR = 8
SKEL = 128
SLOTS = 2
LEAF_DEV = 4
REACH = 3
LEAVES = 256
NODES = LEAVES // LEAF_DEV
RIDGE = 0.1
RATE = 0.25

AUG = 16
PACK = LEAF_PTS + DIMS * LEAF_PTS // 128
OFFSETS = tuple(range(-REACH, 0)) + tuple(range(1, REACH)) + (NODES // 2,)
CLASSES = len(OFFSETS)
T_OK = 0
T_OWN = 8
T_FAR = 32
T_LEN = 128

VMEM = pltpu.VMEM
SMEM = pltpu.SMEM
F32 = jnp.float32
BF16 = jnp.bfloat16
HIGHEST = lax.Precision.HIGHEST


def vm(count):
    return [pl.BlockSpec(memory_space=VMEM)] * count


def dot_tn(a, b):
    return lax.dot_general(a, b, (((0,), (0,)), ((), ())), preferred_element_type=F32)


def dot_nt(a, b):
    return lax.dot_general(a, b, (((1,), (1,)), ((), ())), preferred_element_type=F32)


def split_norm(coords):
    norm = RATE * jnp.sum(coords * coords, axis=0, keepdims=True)
    high = norm.astype(BF16).astype(F32)
    rest = norm - high
    middle = rest.astype(BF16).astype(F32)
    low = rest - middle
    return high, middle, low


def left_side(coords):
    high, middle, low = split_norm(coords)
    row = lax.broadcasted_iota(jnp.int32, (DIMS, coords.shape[1]), 0)
    extra = jnp.where(row == 0, -high, jnp.where(row == 1, -middle, jnp.where(row == 2, -low, jnp.where(row < 6, 1.0, 0.0))))
    return jnp.concatenate([coords * (2.0 * RATE), extra], axis=0).astype(BF16)


def right_side(coords):
    high, middle, low = split_norm(coords)
    row = lax.broadcasted_iota(jnp.int32, (DIMS, coords.shape[1]), 0)
    extra = jnp.where(row == 3, -high, jnp.where(row == 4, -middle, jnp.where(row == 5, -low, jnp.where(row < 3, 1.0, 0.0))))
    return jnp.concatenate([coords, extra], axis=0).astype(BF16)


def send_kernel(near_s, order_s, near_v, points, omega, pivots, table, left, skeleton, *rest):
    packs, turned = rest[:CLASSES], rest[CLASSES:]
    me = lax.axis_index("leaf")
    column = lax.axis_index("samp")
    near = near_v[...]

    def look(k, tree):
        return jnp.where(near == k, order_s[k], tree)

    tree = lax.fori_loop(0, LEAVES, look, jnp.zeros((NEAR, LEAVES), jnp.int32), unroll=8)
    node = lax.broadcasted_iota(jnp.int32, (NEAR, LEAVES), 1) >> 2
    place = ((tree >> 2) - node + REACH) & (NODES - 1)
    bad = jnp.logical_and(place >= 2 * REACH, place != REACH + NODES // 2)
    table[T_OK] = jnp.where(jnp.max(jnp.where(bad, 1.0, 0.0)) > 0.0, 0, 1)

    def wanted(requester):
        mask = jnp.int32(0)
        for member in range(LEAF_DEV):
            for entry in range(NEAR):
                leaf = order_s[near_s[entry, requester * LEAF_DEV + member]]
                mask = mask | jnp.where((leaf >> 2) == me, jnp.int32(1) << (leaf & 3), 0)
        return mask

    def lowest(mask):
        return jnp.where(mask & 1, 0, jnp.where(mask & 2, 1, jnp.where(mask & 4, 2, jnp.where(mask & 8, 3, 0))))

    def highest(mask):
        return jnp.where(mask & 8, 3, jnp.where(mask & 4, 2, jnp.where(mask & 2, 1, 0)))

    for index, offset in enumerate(OFFSETS):
        mask = wanted((me - offset) & (NODES - 1))
        for slot, leaf in enumerate((lowest(mask), highest(mask))):
            packs[index][slot, 0:LEAF_PTS, :] = omega[leaf]
            mine = points[:, pl.ds(pl.multiple_of(leaf * LEAF_PTS, LEAF_PTS), LEAF_PTS)]
            for piece in range(LEAF_PTS // 128):
                packs[index][slot, LEAF_PTS + DIMS * piece:LEAF_PTS + DIMS * (piece + 1), :] = mine[:, 128 * piece:128 * (piece + 1)]

    masks = []
    for member in range(LEAF_DEV):
        mask = jnp.int32(0)
        for entry in range(NEAR):
            leaf = order_s[near_s[entry, me * LEAF_DEV + member]]
            spot = ((leaf >> 2) - me + REACH) & (NODES - 1)
            spot = jnp.where(spot < 2 * REACH, spot, 2 * REACH)
            mask = mask | (jnp.int32(1) << (4 * spot + (leaf & 3)))
        masks.append(mask)
    every = masks[0] | masks[1] | masks[2] | masks[3]
    for member in range(LEAF_DEV):
        for source in range(LEAF_DEV):
            table[T_OWN + LEAF_DEV * member + source] = (masks[member] >> (4 * REACH + source)) & 1
    for index, offset in enumerate(OFFSETS):
        spot = 2 * REACH if offset == NODES // 2 else offset + REACH
        four = (every >> (4 * spot)) & 15
        first, second = lowest(four), highest(four)
        for member in range(LEAF_DEV):
            bits = masks[member] >> (4 * spot)
            table[T_FAR + 8 * index + 2 * member] = (bits >> first) & 1
            table[T_FAR + 8 * index + 2 * member + 1] = jnp.where(first == second, 0, (bits >> second) & 1)

    for member in range(LEAF_DEV):
        coords = points[:, member * LEAF_PTS:(member + 1) * LEAF_PTS]
        left[:, member * LEAF_PTS:(member + 1) * LEAF_PTS] = left_side(coords.astype(F32))
        chosen = lax.broadcasted_iota(jnp.int32, (LEAF_PTS, SKEL), 0) == pivots[member:member + 1, :]
        picked = jnp.dot(coords, jnp.where(chosen, 1.0, 0.0).astype(BF16), preferred_element_type=F32)
        skeleton[:, member * SKEL:(member + 1) * SKEL] = picked.astype(BF16)
    for step in range(1, 4):
        turned[step - 1][...] = omega[(column + step) & 3]


def add_tile(left, right, samples, total, member):
    half = LEAF_PTS // 2

    def rows(part, carry):
        start = pl.multiple_of(member * LEAF_PTS + part * half, half)
        exponent = dot_tn(left[:, pl.ds(start, half)], right)
        tile = jnp.exp(exponent).astype(BF16)
        where = pl.ds(pl.multiple_of(part * half, half), half)
        total[member, where, :] += jnp.dot(tile, samples, preferred_element_type=F32)
        return carry

    lax.fori_loop(0, 2, rows, 0)


def own_kernel(table, left, points, omega, total):
    total[...] = jnp.zeros_like(total)

    def source_step(source, carry):
        coords = points[:, pl.ds(pl.multiple_of(source * LEAF_PTS, LEAF_PTS), LEAF_PTS)]
        right = right_side(coords.astype(F32))
        samples = omega[source]

        def member_step(member, inner):
            @pl.when(table[T_OWN + LEAF_DEV * member + source] > 0)
            def _():
                add_tile(left, right, samples, total, member)
            return inner

        return lax.fori_loop(0, LEAF_DEV, member_step, carry)

    lax.fori_loop(0, LEAF_DEV, source_step, 0)


def far_kernel(index, last, table, left, pack, before, total, *blocks):
    total[...] = before[...]

    def slot_step(slot, carry):
        pieces = [pack[slot, LEAF_PTS + DIMS * c:LEAF_PTS + DIMS * (c + 1), :] for c in range(LEAF_PTS // 128)]
        coords = jnp.concatenate([p.astype(F32) for p in pieces], axis=1)
        right = right_side(coords)
        samples = pack[slot, 0:LEAF_PTS, :]

        def member_step(member, inner):
            @pl.when(table[T_FAR + 8 * index + 2 * member + slot] > 0)
            def _():
                add_tile(left, right, samples, total, member)
            return inner

        return lax.fori_loop(0, LEAF_DEV, member_step, carry)

    lax.fori_loop(0, SLOTS, slot_step, 0)
    if last:
        column = lax.axis_index("samp")
        for step in range(4):
            blocks[step][...] = total[(column + step) & 3].astype(BF16)


def rows_kernel(total, pivots, skeleton, sibling, rows, coupling):
    for member in range(LEAF_DEV):
        chosen = lax.broadcasted_iota(jnp.int32, (LEAF_PTS, SKEL), 0) == pivots[member:member + 1, :]
        pick = jnp.where(chosen, 1.0, 0.0)
        values = total[member]
        rows[member * SKEL:(member + 1) * SKEL, :] = lax.dot_general(pick, values, (((0,), (0,)), ((), ())), preferred_element_type=F32, precision=HIGHEST)
    exponent = dot_tn(left_side(skeleton[...].astype(F32)), right_side(sibling[...].astype(F32)))
    coupling[...] = jnp.exp(exponent).astype(BF16)


def matmul3(a, b):
    a_high = a.astype(BF16)
    a_low = (a - a_high.astype(F32)).astype(BF16)
    b_high = b.astype(BF16)
    b_low = (b - b_high.astype(F32)).astype(BF16)
    dot = functools.partial(jnp.dot, preferred_element_type=F32)
    return dot(a_high, b_high) + (dot(a_high, b_low) + dot(a_low, b_high))


def inverse(gram):
    row = lax.broadcasted_iota(jnp.int32, (SKEL, SKEL), 0)
    eye = jnp.where(row == lax.broadcasted_iota(jnp.int32, (SKEL, SKEL), 1), 1.0, 0.0)
    trace = jnp.sum(jnp.sum(gram * eye, axis=1, keepdims=True), axis=0, keepdims=True)
    shift = RIDGE * trace / SKEL
    scaled = gram / shift + eye
    spread = 1.0 + SKEL / RIDGE
    error = (spread - 1.0) / (spread + 1.0)
    start = 2.0 / (1.0 + spread)
    guess = start * (2.0 * eye - start * scaled)
    error = error * error
    steps = 0
    while error > 1e-9:
        factor = 2.0 / (2.0 - error)
        guess = guess * factor
        error = error / (2.0 - error)
        late = error < 0.1
        multiply = functools.partial(jnp.dot, precision=HIGHEST, preferred_element_type=F32) if late else matmul3
        guess = 2.0 * guess - multiply(guess, multiply(scaled, guess))
        error = error * error
        steps += 1
    return guess / shift


def solve_kernel(b0, b1, b2, b3, pivots, o0, o1, o2, o3, interpolation, p0, p1, p2, p3):
    column = lax.axis_index("samp")
    mine = pivots[pl.ds(column, 1), :]
    chosen = lax.broadcasted_iota(jnp.int32, (LEAF_PTS, SKEL), 0) == mine
    pick = jnp.where(chosen, 1.0, 0.0).astype(BF16)
    gram = jnp.zeros((SKEL, SKEL), F32)
    cross = jnp.zeros((LEAF_PTS, SKEL), F32)
    for block in (b0, b1, b2, b3):
        values = block[...]
        rows = dot_tn(pick, values).astype(BF16)
        gram += dot_nt(rows, rows)
        cross += dot_nt(values, rows)
    result = jnp.dot(cross, inverse(gram), precision=HIGHEST, preferred_element_type=F32).astype(BF16)
    interpolation[...] = result
    for block, out in ((o0, p0), (o1, p1), (o2, p2), (o3, p3)):
        out[...] = dot_tn(result, block[...]).astype(BF16)


def final_kernel(rows, coupling, q0, q1, q2, q3, i0, i1, i2, i3, interpolation, parent, stack):
    column = lax.axis_index("samp")
    for step, block in enumerate((q0, q1, q2, q3)):
        leaf = (column + step) & 3
        stack[pl.ds(pl.multiple_of(leaf * SKEL, SKEL), SKEL), :] = block[...]
    parent[...] = rows[...] - jnp.dot(coupling[...], stack[...], preferred_element_type=F32)
    for step, block in enumerate((i0, i1, i2, i3)):
        leaf = (column - step) & 3
        interpolation[pl.ds(pl.multiple_of(leaf * LEAF_PTS, LEAF_PTS), LEAF_PTS), :] = block[...]


def general_sample(points, omega, near_lists, leaf_order):
    nodes = lax.axis_size("leaf")
    me = lax.axis_index("leaf")
    columns = omega.shape[1]
    references = LEAF_DEV * NEAR
    tree = jnp.take(leaf_order, near_lists, axis=0).reshape(nodes, references)
    leaf = lax.broadcasted_iota(jnp.int32, (1, 1, LEAF_DEV), 2)
    wants = jnp.any(tree[:, :, None] == me * LEAF_DEV + leaf, axis=1)
    first = jnp.argmax(wants, axis=1).astype(jnp.int32)
    second = (LEAF_DEV - 1 - jnp.argmax(wants[:, ::-1], axis=1)).astype(jnp.int32)
    send = jnp.stack([first, second], axis=1).reshape(-1)
    leaf_points = jnp.moveaxis(points.reshape(DIMS, LEAF_DEV, LEAF_PTS), 1, 0)
    got_points = lax.all_to_all(jnp.take(leaf_points, send, axis=0), "leaf", 0, 0, tiled=True)
    got_samples = lax.all_to_all(jnp.take(omega.reshape(LEAF_DEV, LEAF_PTS, columns), send, axis=0), "leaf", 0, 0, tiled=True)
    mine = lax.dynamic_index_in_dim(tree, me, 0, keepdims=False)
    smaller = jnp.any(jnp.logical_and((mine[:, None] >> 2) == (mine[None, :] >> 2), mine[None, :] < mine[:, None]), axis=1)
    arrival = ((mine >> 2) * SLOTS + smaller.astype(jnp.int32)).reshape(LEAF_DEV, NEAR)

    def one(member):
        slots = lax.dynamic_index_in_dim(arrival, member, 0, keepdims=False)
        far = jnp.moveaxis(jnp.take(got_points, slots, axis=0), 0, 1).reshape(DIMS, NEAR * LEAF_PTS)
        samples = jnp.take(got_samples, slots, axis=0).reshape(NEAR * LEAF_PTS, columns)
        own = lax.dynamic_index_in_dim(leaf_points, member, 0, keepdims=False)
        own_f, far_f = own.astype(F32), far.astype(F32)
        inner = jnp.dot(own.T, far, preferred_element_type=F32)
        distance = jnp.sum(own_f * own_f, 0)[:, None] + jnp.sum(far_f * far_f, 0)[None, :] - 2.0 * inner
        return jnp.dot(jnp.exp(-RATE * distance).astype(BF16), samples, preferred_element_type=F32)

    return lax.map(one, jnp.arange(LEAF_DEV, dtype=jnp.int32))


def shards(points, omega, near_lists, leaf_order, pivots):
    columns = omega.shape[1]
    near = near_lists.T
    leaves = omega.reshape(LEAF_DEV, LEAF_PTS, columns)
    shape = jax.ShapeDtypeStruct
    block = shape((LEAF_PTS, columns), BF16)
    smem = pl.BlockSpec(memory_space=SMEM)
    sent = pl.pallas_call(
        send_kernel,
        name="send",
        out_shape=[shape((T_LEN,), jnp.int32), shape((AUG, LEAF_DEV * LEAF_PTS), BF16), shape((DIMS, LEAF_DEV * SKEL), BF16)]
        + [shape((SLOTS, PACK, columns), BF16)] * CLASSES + [block] * 3,
        in_specs=[smem, smem] + vm(4),
        out_specs=[smem] + vm(2 + CLASSES + 3),
    )(near, leaf_order, near, points, leaves, pivots)
    table, left, skeleton = sent[:3]
    packs, turned = sent[3:3 + CLASSES], sent[3 + CLASSES:]

    both = ("leaf", "samp")
    sibling = lax.ppermute(skeleton, "leaf", [(n, n ^ 1) for n in range(NODES)])
    turned_in = [lax.ppermute(t, "samp", [(s, (s + k) % 4) for s in range(4)]) for k, t in enumerate(turned, 1)]
    turned_own = lax.dynamic_index_in_dim(leaves, lax.axis_index("samp"), 0, keepdims=False)

    total_shape = shape((LEAF_DEV, LEAF_PTS, columns), F32)

    def near_branch(points, leaves, near_lists, leaf_order, table, left, packs):
        arrived = [
            lax.ppermute(pack, "leaf", [((n + offset) % NODES, n) for n in range(NODES)])
            for pack, offset in zip(packs, OFFSETS)
        ]
        total = pl.pallas_call(
            own_kernel, name="own", out_shape=total_shape, in_specs=[smem] + vm(3), out_specs=pl.BlockSpec(memory_space=VMEM)
        )(table, left, points, leaves)
        for index in range(CLASSES):
            last = index == CLASSES - 1
            out = pl.pallas_call(
                functools.partial(far_kernel, index, last),
                name=f"far{index}",
                out_shape=[total_shape] + ([block] * 4 if last else []),
                in_specs=[smem] + vm(3),
                out_specs=vm(5 if last else 1),
                input_output_aliases={3: 0},
            )(table, left, arrived[index], total)
            total = out[0]
        return total, tuple(out[1:])

    def any_branch(points, leaves, near_lists, leaf_order, table, left, packs):
        total = general_sample(points, leaves.reshape(-1, columns), near_lists, leaf_order)
        column = lax.axis_index("samp")
        return total, tuple(
            lax.dynamic_index_in_dim(total, (column + k) & 3, 0, keepdims=False).astype(BF16) for k in range(4)
        )

    total, blocks = lax.cond(
        table[T_OK] > 0, near_branch, any_branch, points, leaves, near_lists, leaf_order, table, left, packs
    )
    swapped = [blocks[0]] + [
        lax.ppermute(blocks[k], "samp", [(s, (s + k) % 4) for s in range(4)]) for k in range(1, 4)
    ]
    rows, coupling = pl.pallas_call(
        rows_kernel,
        name="rows",
        out_shape=[shape((LEAF_DEV * SKEL, columns), F32), shape((LEAF_DEV * SKEL, LEAF_DEV * SKEL), BF16)],
        in_specs=vm(4),
        out_specs=vm(2),
    )(total, pivots, skeleton, sibling)
    small = shape((SKEL, columns), BF16)
    interpolation, *projected = pl.pallas_call(
        solve_kernel,
        name="solve",
        out_shape=[shape((LEAF_PTS, SKEL), BF16)] + [small] * 4,
        in_specs=vm(9),
        out_specs=vm(5),
    )(*swapped, pivots, turned_own, *turned_in)
    crossed = [
        lax.ppermute(
            projected[k], both, [(n * 4 + s, (n ^ 1) * 4 + (s - k) % 4) for n in range(NODES) for s in range(4)]
        )
        for k in range(4)
    ]
    spread = [interpolation] + [
        lax.ppermute(interpolation, "samp", [(s, (s + k) % 4) for s in range(4)]) for k in range(1, 4)
    ]
    return tuple(
        pl.pallas_call(
            final_kernel,
            name="final",
            out_shape=[shape((LEAF_DEV * LEAF_PTS, SKEL), BF16), shape((LEAF_DEV * SKEL, columns), F32)],
            in_specs=vm(10),
            out_specs=vm(2),
            scratch_shapes=[pltpu.VMEM((LEAF_DEV * SKEL, columns), BF16)],
        )(rows, coupling, *crossed, *spread)
    )


def solution(mesh):
    placed = (P(None, "leaf"), P("leaf", "samp"), P(), P(), P("leaf", None))
    return jax.shard_map(
        shards,
        mesh=mesh,
        in_specs=placed,
        out_specs=(P("leaf", None), P("leaf", "samp")),
        check_vma=False,
    )
```

```python
import functools

import jax
import jax.numpy as jnp
from jax import lax
from jax.experimental import pallas as pl
from jax.experimental.pallas import tpu as pltpu
from jax.sharding import PartitionSpec as P

DIMS = 8
LEAF_PTS = 512
NEAR = 8
SKEL = 128
SLOTS = 2
LEAF_DEV = 4
REACH = 3
LEAVES = 256
NODES = LEAVES // LEAF_DEV
RIDGE = 0.1
RATE = 0.25

AUG = 16
PACK = LEAF_PTS + DIMS * LEAF_PTS // 128
OFFSETS = tuple(range(-REACH, 0)) + tuple(range(1, REACH)) + (NODES // 2,)
CLASSES = len(OFFSETS)
T_OK = 0
T_OWN = 8
T_FAR = 32
T_LEN = 128
VMEM_LIMIT = 16 << 20

VMEM = pltpu.VMEM
SMEM = pltpu.SMEM
F32 = jnp.float32
BF16 = jnp.bfloat16
HIGHEST = lax.Precision.HIGHEST


def vm(count):
    return [pl.BlockSpec(memory_space=VMEM)] * count


def dot_tn(a, b):
    return lax.dot_general(a, b, (((0,), (0,)), ((), ())), preferred_element_type=F32)


def dot_nt(a, b):
    return lax.dot_general(a, b, (((1,), (1,)), ((), ())), preferred_element_type=F32)


def split_norm(coords):
    norm = RATE * jnp.sum(coords * coords, axis=0, keepdims=True)
    high = norm.astype(BF16).astype(F32)
    rest = norm - high
    middle = rest.astype(BF16).astype(F32)
    low = rest - middle
    return high, middle, low


def left_side(coords):
    high, middle, low = split_norm(coords)
    row = lax.broadcasted_iota(jnp.int32, (DIMS, coords.shape[1]), 0)
    extra = jnp.where(row == 0, -high, jnp.where(row == 1, -middle, jnp.where(row == 2, -low, jnp.where(row < 6, 1.0, 0.0))))
    return jnp.concatenate([coords * (2.0 * RATE), extra], axis=0).astype(BF16)


def right_side(coords):
    high, middle, low = split_norm(coords)
    row = lax.broadcasted_iota(jnp.int32, (DIMS, coords.shape[1]), 0)
    extra = jnp.where(row == 3, -high, jnp.where(row == 4, -middle, jnp.where(row == 5, -low, jnp.where(row < 3, 1.0, 0.0))))
    return jnp.concatenate([coords, extra], axis=0).astype(BF16)


def send_kernel(near_s, order_s, near_v, points, omega, table, *packs):
    me = lax.axis_index("leaf")
    near = near_v[...]

    def look(k, tree):
        return jnp.where(near == k, order_s[k], tree)

    tree = lax.fori_loop(0, LEAVES, look, jnp.zeros((NEAR, LEAVES), jnp.int32), unroll=16)
    node = lax.broadcasted_iota(jnp.int32, (NEAR, LEAVES), 1) >> 2
    part = tree & 3
    weight = jnp.where(part == 0, 1.0, jnp.where(part == 1, 8.0, jnp.where(part == 2, 64.0, 512.0)))
    weight = jnp.where((tree >> 2) == me, weight, 0.0)
    for index, offset in enumerate(OFFSETS):
        requester = (me - offset) & (NODES - 1)
        counts = jnp.sum(jnp.where(node == requester, weight, 0.0)).astype(jnp.int32)
        has = [(counts >> (3 * leaf)) & 7 > 0 for leaf in range(LEAF_DEV)]
        first = jnp.where(has[0], 0, jnp.where(has[1], 1, jnp.where(has[2], 2, jnp.where(has[3], 3, 0))))
        second = jnp.where(has[3], 3, jnp.where(has[2], 2, jnp.where(has[1], 1, 0)))
        for slot, leaf in enumerate((first, second)):
            packs[index][slot, 0:LEAF_PTS, :] = omega[leaf]
            mine = points[:, pl.ds(pl.multiple_of(leaf * LEAF_PTS, LEAF_PTS), LEAF_PTS)]
            for piece in range(LEAF_PTS // 128):
                packs[index][slot, LEAF_PTS + DIMS * piece:LEAF_PTS + DIMS * (piece + 1), :] = mine[:, 128 * piece:128 * (piece + 1)]

    place = ((tree >> 2) - node + REACH) & (NODES - 1)
    bad = jnp.logical_and(place >= 2 * REACH, place != REACH + NODES // 2)
    table[T_OK] = jnp.where(jnp.max(jnp.where(bad, 1.0, 0.0)) > 0.0, 0, 1)

    def lowest(mask):
        return jnp.where(mask & 1 > 0, 0, jnp.where(mask & 2 > 0, 1, jnp.where(mask & 4 > 0, 2, jnp.where(mask & 8 > 0, 3, 0))))

    def highest(mask):
        return jnp.where(mask & 8 > 0, 3, jnp.where(mask & 4 > 0, 2, jnp.where(mask & 2 > 0, 1, 0)))

    masks = []
    for member in range(LEAF_DEV):
        mask = jnp.int32(0)
        for entry in range(NEAR):
            leaf = order_s[near_s[entry, me * LEAF_DEV + member]]
            spot = ((leaf >> 2) - me + REACH) & (NODES - 1)
            spot = jnp.where(spot < 2 * REACH, spot, 2 * REACH)
            mask = mask | (jnp.int32(1) << (4 * spot + (leaf & 3)))
        masks.append(mask)
    every = masks[0] | masks[1] | masks[2] | masks[3]
    for member in range(LEAF_DEV):
        for source in range(LEAF_DEV):
            table[T_OWN + LEAF_DEV * member + source] = (masks[member] >> (4 * REACH + source)) & 1
    for index, offset in enumerate(OFFSETS):
        spot = 2 * REACH if offset == NODES // 2 else offset + REACH
        four = (every >> (4 * spot)) & 15
        first, second = lowest(four), highest(four)
        for member in range(LEAF_DEV):
            bits = masks[member] >> (4 * spot)
            table[T_FAR + 8 * index + 2 * member] = (bits >> first) & 1
            table[T_FAR + 8 * index + 2 * member + 1] = jnp.where(first == second, 0, (bits >> second) & 1)


def add_tile(left, right, samples, total, member):
    start = pl.multiple_of(member * LEAF_PTS, LEAF_PTS)
    exponent = jnp.dot(left[pl.ds(start, LEAF_PTS), :], right, preferred_element_type=F32)
    tile = jnp.exp(exponent).astype(BF16)
    total[member] += jnp.dot(tile, samples, preferred_element_type=F32)


def own_kernel(table, points, omega, pivots, total, left, skeleton, *turned):
    column = lax.axis_index("samp")
    for member in range(LEAF_DEV):
        coords = points[:, member * LEAF_PTS:(member + 1) * LEAF_PTS]
        left[member * LEAF_PTS:(member + 1) * LEAF_PTS, :] = left_side(coords.astype(F32)).astype(F32).T.astype(BF16)
        chosen = lax.broadcasted_iota(jnp.int32, (LEAF_PTS, SKEL), 0) == pivots[member:member + 1, :]
        picked = jnp.dot(coords, jnp.where(chosen, 1.0, 0.0).astype(BF16), preferred_element_type=F32)
        skeleton[:, member * SKEL:(member + 1) * SKEL] = picked.astype(BF16)
    for step in range(4):
        turned[step][...] = omega[(column + step) & 3]
    total[...] = jnp.zeros_like(total)

    def source_step(source, carry):
        coords = points[:, pl.ds(pl.multiple_of(source * LEAF_PTS, LEAF_PTS), LEAF_PTS)]
        right = right_side(coords.astype(F32))
        samples = omega[source]

        def member_step(member, inner):
            @pl.when(table[T_OWN + LEAF_DEV * member + source] > 0)
            def _():
                add_tile(left, right, samples, total, member)
            return inner

        return lax.fori_loop(0, LEAF_DEV, member_step, carry)

    lax.fori_loop(0, LEAF_DEV, source_step, 0)


def far_kernel(index, last, table, left, pack, before, total, *blocks):
    total[...] = before[...]

    def slot_step(slot, carry):
        pieces = [pack[slot, LEAF_PTS + DIMS * c:LEAF_PTS + DIMS * (c + 1), :] for c in range(LEAF_PTS // 128)]
        coords = jnp.concatenate([p.astype(F32) for p in pieces], axis=1)
        right = right_side(coords)
        samples = pack[slot, 0:LEAF_PTS, :]

        def member_step(member, inner):
            @pl.when(table[T_FAR + 8 * index + 2 * member + slot] > 0)
            def _():
                add_tile(left, right, samples, total, member)
            return inner

        return lax.fori_loop(0, LEAF_DEV, member_step, carry)

    lax.fori_loop(0, SLOTS, slot_step, 0)
    if last:
        column = lax.axis_index("samp")
        for step in range(4):
            blocks[step][...] = total[(column + step) & 3].astype(BF16)


def rows_kernel(total, pivots, skeleton, sibling, rows, coupling):
    for member in range(LEAF_DEV):
        chosen = lax.broadcasted_iota(jnp.int32, (LEAF_PTS, SKEL), 0) == pivots[member:member + 1, :]
        pick = jnp.where(chosen, 1.0, 0.0)
        values = total[member]
        rows[member * SKEL:(member + 1) * SKEL, :] = lax.dot_general(pick, values, (((0,), (0,)), ((), ())), preferred_element_type=F32, precision=HIGHEST)
    exponent = dot_tn(left_side(skeleton[...].astype(F32)), right_side(sibling[...].astype(F32)))
    coupling[...] = jnp.exp(exponent).astype(BF16)


def matmul3(a, b):
    a_high = a.astype(BF16)
    a_low = (a - a_high.astype(F32)).astype(BF16)
    b_high = b.astype(BF16)
    b_low = (b - b_high.astype(F32)).astype(BF16)
    dot = functools.partial(jnp.dot, preferred_element_type=F32)
    return dot(a_high, b_high) + (dot(a_high, b_low) + dot(a_low, b_high))


def inverse(gram):
    row = lax.broadcasted_iota(jnp.int32, (SKEL, SKEL), 0)
    eye = jnp.where(row == lax.broadcasted_iota(jnp.int32, (SKEL, SKEL), 1), 1.0, 0.0)
    trace = jnp.sum(jnp.sum(gram * eye, axis=1, keepdims=True), axis=0, keepdims=True)
    shift = RIDGE * trace / SKEL
    scaled = gram / shift + eye
    spread = 1.0 + SKEL / RIDGE
    error = (spread - 1.0) / (spread + 1.0)
    start = 2.0 / (1.0 + spread)
    guess = start * (2.0 * eye - start * scaled)
    error = error * error
    steps = 0
    while error > 1e-9:
        factor = 2.0 / (2.0 - error)
        guess = guess * factor
        error = error / (2.0 - error)
        late = error < 0.1
        multiply = functools.partial(jnp.dot, precision=HIGHEST, preferred_element_type=F32) if late else matmul3
        guess = 2.0 * guess - multiply(guess, multiply(scaled, guess))
        error = error * error
        steps += 1
    return guess / shift


def solve_kernel(b0, b1, b2, b3, pivots, o0, o1, o2, o3, rows, coupling, interpolation, p0, p1, p2, p3):
    del rows, coupling
    column = lax.axis_index("samp")
    mine = pivots[pl.ds(column, 1), :]
    chosen = lax.broadcasted_iota(jnp.int32, (LEAF_PTS, SKEL), 0) == mine
    pick = jnp.where(chosen, 1.0, 0.0).astype(BF16)
    gram = jnp.zeros((SKEL, SKEL), F32)
    cross = jnp.zeros((LEAF_PTS, SKEL), F32)
    for block in (b0, b1, b2, b3):
        values = block[...]
        rows = dot_tn(pick, values).astype(BF16)
        gram += dot_nt(rows, rows)
        cross += dot_nt(values, rows)
    result = jnp.dot(cross, inverse(gram), precision=HIGHEST, preferred_element_type=F32).astype(BF16)
    interpolation[...] = result
    for block, out in ((o0, p0), (o1, p1), (o2, p2), (o3, p3)):
        out[...] = dot_tn(result, block[...]).astype(BF16)


def final_kernel(rows, coupling, q0, q1, q2, q3, i0, i1, i2, i3, interpolation, parent, stack):
    column = lax.axis_index("samp")
    for step, block in enumerate((q0, q1, q2, q3)):
        leaf = (column + step) & 3
        stack[pl.ds(pl.multiple_of(leaf * SKEL, SKEL), SKEL), :] = block[...]
    parent[...] = rows[...] - jnp.dot(coupling[...], stack[...], preferred_element_type=F32)
    for step, block in enumerate((i0, i1, i2, i3)):
        leaf = (column - step) & 3
        interpolation[pl.ds(pl.multiple_of(leaf * LEAF_PTS, LEAF_PTS), LEAF_PTS), :] = block[...]


def general_sample(points, omega, near_lists, leaf_order):
    nodes = lax.axis_size("leaf")
    me = lax.axis_index("leaf")
    columns = omega.shape[1]
    references = LEAF_DEV * NEAR
    tree = jnp.take(leaf_order, near_lists, axis=0).reshape(nodes, references)
    leaf = lax.broadcasted_iota(jnp.int32, (1, 1, LEAF_DEV), 2)
    wants = jnp.any(tree[:, :, None] == me * LEAF_DEV + leaf, axis=1)
    first = jnp.argmax(wants, axis=1).astype(jnp.int32)
    second = (LEAF_DEV - 1 - jnp.argmax(wants[:, ::-1], axis=1)).astype(jnp.int32)
    send = jnp.stack([first, second], axis=1).reshape(-1)
    leaf_points = jnp.moveaxis(points.reshape(DIMS, LEAF_DEV, LEAF_PTS), 1, 0)
    got_points = lax.all_to_all(jnp.take(leaf_points, send, axis=0), "leaf", 0, 0, tiled=True)
    got_samples = lax.all_to_all(jnp.take(omega.reshape(LEAF_DEV, LEAF_PTS, columns), send, axis=0), "leaf", 0, 0, tiled=True)
    mine = lax.dynamic_index_in_dim(tree, me, 0, keepdims=False)
    smaller = jnp.any(jnp.logical_and((mine[:, None] >> 2) == (mine[None, :] >> 2), mine[None, :] < mine[:, None]), axis=1)
    arrival = ((mine >> 2) * SLOTS + smaller.astype(jnp.int32)).reshape(LEAF_DEV, NEAR)

    def one(member):
        slots = lax.dynamic_index_in_dim(arrival, member, 0, keepdims=False)
        far = jnp.moveaxis(jnp.take(got_points, slots, axis=0), 0, 1).reshape(DIMS, NEAR * LEAF_PTS)
        samples = jnp.take(got_samples, slots, axis=0).reshape(NEAR * LEAF_PTS, columns)
        own = lax.dynamic_index_in_dim(leaf_points, member, 0, keepdims=False)
        own_f, far_f = own.astype(F32), far.astype(F32)
        inner = jnp.dot(own.T, far, preferred_element_type=F32)
        distance = jnp.sum(own_f * own_f, 0)[:, None] + jnp.sum(far_f * far_f, 0)[None, :] - 2.0 * inner
        return jnp.dot(jnp.exp(-RATE * distance).astype(BF16), samples, preferred_element_type=F32)

    return lax.map(one, jnp.arange(LEAF_DEV, dtype=jnp.int32))


def call(kernel, name, out_shape, in_specs, out_specs, **more):
    return pl.pallas_call(
        kernel,
        name=name,
        out_shape=out_shape,
        in_specs=in_specs,
        out_specs=out_specs,
        compiler_params=pltpu.CompilerParams(vmem_limit_bytes=VMEM_LIMIT),
        **more,
    )


def shards(points, omega, near_lists, leaf_order, pivots):
    columns = omega.shape[1]
    near = near_lists.T
    leaves = omega.reshape(LEAF_DEV, LEAF_PTS, columns)
    shape = jax.ShapeDtypeStruct
    block = shape((LEAF_PTS, columns), BF16)
    smem = pl.BlockSpec(memory_space=SMEM)
    anywhere = pl.BlockSpec(memory_space=pl.ANY)
    table, *packs = call(
        send_kernel,
        "send",
        [shape((T_LEN,), jnp.int32)] + [shape((SLOTS, PACK, columns), BF16)] * CLASSES,
        [smem, smem] + vm(3),
        [smem] + vm(CLASSES),
    )(near, leaf_order, near, points, leaves)

    both = ("leaf", "samp")
    total_shape = shape((LEAF_DEV, LEAF_PTS, columns), F32)

    def shift(value, k):
        return lax.ppermute(value, "samp", [(s, (s + k) % 4) for s in range(4)])

    def own(points, leaves, table, pivots):
        total, left, skeleton, *turned = call(
            own_kernel,
            "own",
            [total_shape, shape((LEAF_DEV * LEAF_PTS, AUG), BF16), shape((DIMS, LEAF_DEV * SKEL), BF16)] + [block] * 4,
            [smem] + vm(3),
            vm(7),
        )(table, points, leaves, pivots)
        sibling = lax.ppermute(skeleton, "leaf", [(n, n ^ 1) for n in range(NODES)])
        turned = [turned[0]] + [shift(turned[k], k) for k in range(1, 4)]
        return total, left, skeleton, sibling, turned

    def near_branch(points, leaves, near_lists, leaf_order, pivots, table, packs):
        arrived = [
            lax.ppermute(pack, "leaf", [((n + offset) % NODES, n) for n in range(NODES)])
            for pack, offset in zip(packs, OFFSETS)
        ]
        total, left, skeleton, sibling, turned = own(points, leaves, table, pivots)
        for index in range(CLASSES):
            last = index == CLASSES - 1
            total, *blocks = call(
                functools.partial(far_kernel, index, last),
                f"far{index}",
                [total_shape] + ([block] * 4 if last else []),
                [smem] + vm(3),
                vm(5 if last else 1),
                input_output_aliases={3: 0},
            )(table, left, arrived[index], total)
        return total, blocks, skeleton, sibling, turned

    def any_branch(points, leaves, near_lists, leaf_order, pivots, table, packs):
        total = general_sample(points, leaves.reshape(-1, columns), near_lists, leaf_order)
        column = lax.axis_index("samp")
        blocks = [lax.dynamic_index_in_dim(total, (column + k) & 3, 0, keepdims=False).astype(BF16) for k in range(4)]
        return total, blocks, *own(points, leaves, table, pivots)[2:]

    total, blocks, skeleton, sibling, turned = lax.cond(
        table[T_OK] > 0, near_branch, any_branch, points, leaves, near_lists, leaf_order, pivots, table, packs
    )
    swapped = [blocks[0]] + [shift(blocks[k], k) for k in range(1, 4)]
    rows, coupling = call(
        rows_kernel,
        "rows",
        [shape((LEAF_DEV * SKEL, columns), F32), shape((LEAF_DEV * SKEL, LEAF_DEV * SKEL), BF16)],
        vm(4),
        vm(2),
    )(total, pivots, skeleton, sibling)
    small = shape((SKEL, columns), BF16)
    interpolation, *projected = call(
        solve_kernel,
        "solve",
        [shape((LEAF_PTS, SKEL), BF16)] + [small] * 4,
        vm(9) + [anywhere] * 2,
        vm(5),
    )(*swapped, pivots, *turned, rows, coupling)
    crossed = [
        lax.ppermute(
            projected[k], both, [(n * 4 + s, (n ^ 1) * 4 + (s - k) % 4) for n in range(NODES) for s in range(4)]
        )
        for k in range(4)
    ]
    spread = [interpolation] + [shift(interpolation, k) for k in range(1, 4)]
    return tuple(
        call(
            final_kernel,
            "final",
            [shape((LEAF_DEV * LEAF_PTS, SKEL), BF16), shape((LEAF_DEV * SKEL, columns), F32)],
            vm(10),
            vm(2),
            scratch_shapes=[pltpu.VMEM((LEAF_DEV * SKEL, columns), BF16)],
        )(rows, coupling, *crossed, *spread)
    )


def solution(mesh):
    placed = (P(None, "leaf"), P("leaf", "samp"), P(), P(), P("leaf", None))
    return jax.shard_map(
        shards,
        mesh=mesh,
        in_specs=placed,
        out_specs=(P("leaf", None), P("leaf", "samp")),
        check_vma=False,
    )
```

```python
import functools

import jax
import jax.numpy as jnp
from jax import lax
from jax.experimental import pallas as pl
from jax.experimental.pallas import tpu as pltpu
from jax.sharding import PartitionSpec as P

DIMS = 8
LEAF_PTS = 512
NEAR = 8
SKEL = 128
SLOTS = 2
LEAF_DEV = 4
REACH = 3
LEAVES = 256
NODES = LEAVES // LEAF_DEV
RIDGE = 0.1
RATE = 0.25

AUG = 16
PACK = LEAF_PTS + DIMS * LEAF_PTS // 128
OFFSETS = tuple(range(-REACH, 0)) + tuple(range(1, REACH)) + (NODES // 2,)
CLASSES = len(OFFSETS)
LATE = (0, CLASSES - 1)
EARLY = tuple(i for i in range(CLASSES) if i not in LATE)
T_OK = 0
T_OWN = 8
T_FAR = 32
T_LEN = 128
VMEM_LIMIT = 16 << 20

VMEM = pltpu.VMEM
SMEM = pltpu.SMEM
F32 = jnp.float32
BF16 = jnp.bfloat16
HIGHEST = lax.Precision.HIGHEST


def vm(count):
    return [pl.BlockSpec(memory_space=VMEM)] * count


def dot_tn(a, b):
    return lax.dot_general(a, b, (((0,), (0,)), ((), ())), preferred_element_type=F32)


def dot_nt(a, b):
    return lax.dot_general(a, b, (((1,), (1,)), ((), ())), preferred_element_type=F32)


def split_norm(coords):
    norm = RATE * jnp.sum(coords * coords, axis=0, keepdims=True)
    high = norm.astype(BF16).astype(F32)
    rest = norm - high
    middle = rest.astype(BF16).astype(F32)
    low = rest - middle
    return high, middle, low


def left_side(coords):
    high, middle, low = split_norm(coords)
    row = lax.broadcasted_iota(jnp.int32, (DIMS, coords.shape[1]), 0)
    extra = jnp.where(row == 0, -high, jnp.where(row == 1, -middle, jnp.where(row == 2, -low, jnp.where(row < 6, 1.0, 0.0))))
    return jnp.concatenate([coords * (2.0 * RATE), extra], axis=0).astype(BF16)


def right_side(coords):
    high, middle, low = split_norm(coords)
    row = lax.broadcasted_iota(jnp.int32, (DIMS, coords.shape[1]), 0)
    extra = jnp.where(row == 3, -high, jnp.where(row == 4, -middle, jnp.where(row == 5, -low, jnp.where(row < 3, 1.0, 0.0))))
    return jnp.concatenate([coords, extra], axis=0).astype(BF16)


def send_kernel(near_s, order_s, near_v, points, omega, table, *packs):
    me = lax.axis_index("leaf")
    near = near_v[...]

    def look(k, tree):
        return jnp.where(near == k, order_s[k], tree)

    tree = lax.fori_loop(0, LEAVES, look, jnp.zeros((NEAR, LEAVES), jnp.int32), unroll=16)
    node = lax.broadcasted_iota(jnp.int32, (NEAR, LEAVES), 1) >> 2
    part = tree & 3
    weight = jnp.where(part == 0, 1.0, jnp.where(part == 1, 8.0, jnp.where(part == 2, 64.0, 512.0)))
    weight = jnp.where((tree >> 2) == me, weight, 0.0)
    for index, offset in enumerate(OFFSETS):
        requester = (me - offset) & (NODES - 1)
        counts = jnp.sum(jnp.where(node == requester, weight, 0.0)).astype(jnp.int32)
        has = [(counts >> (3 * leaf)) & 7 > 0 for leaf in range(LEAF_DEV)]
        first = jnp.where(has[0], 0, jnp.where(has[1], 1, jnp.where(has[2], 2, jnp.where(has[3], 3, 0))))
        second = jnp.where(has[3], 3, jnp.where(has[2], 2, jnp.where(has[1], 1, 0)))
        for slot, leaf in enumerate((first, second)):
            packs[index][slot, 0:LEAF_PTS, :] = omega[leaf]
            mine = points[:, pl.ds(pl.multiple_of(leaf * LEAF_PTS, LEAF_PTS), LEAF_PTS)]
            for piece in range(LEAF_PTS // 128):
                packs[index][slot, LEAF_PTS + DIMS * piece:LEAF_PTS + DIMS * (piece + 1), :] = mine[:, 128 * piece:128 * (piece + 1)]

    place = ((tree >> 2) - node + REACH) & (NODES - 1)
    bad = jnp.logical_and(place >= 2 * REACH, place != REACH + NODES // 2)
    table[T_OK] = jnp.where(jnp.max(jnp.where(bad, 1.0, 0.0)) > 0.0, 0, 1)

    def lowest(mask):
        return jnp.where(mask & 1 > 0, 0, jnp.where(mask & 2 > 0, 1, jnp.where(mask & 4 > 0, 2, jnp.where(mask & 8 > 0, 3, 0))))

    def highest(mask):
        return jnp.where(mask & 8 > 0, 3, jnp.where(mask & 4 > 0, 2, jnp.where(mask & 2 > 0, 1, 0)))

    masks = []
    for member in range(LEAF_DEV):
        mask = jnp.int32(0)
        for entry in range(NEAR):
            leaf = order_s[near_s[entry, me * LEAF_DEV + member]]
            spot = ((leaf >> 2) - me + REACH) & (NODES - 1)
            spot = jnp.where(spot < 2 * REACH, spot, 2 * REACH)
            mask = mask | (jnp.int32(1) << (4 * spot + (leaf & 3)))
        masks.append(mask)
    every = masks[0] | masks[1] | masks[2] | masks[3]
    for member in range(LEAF_DEV):
        for source in range(LEAF_DEV):
            table[T_OWN + LEAF_DEV * member + source] = (masks[member] >> (4 * REACH + source)) & 1
    for index, offset in enumerate(OFFSETS):
        spot = 2 * REACH if offset == NODES // 2 else offset + REACH
        four = (every >> (4 * spot)) & 15
        first, second = lowest(four), highest(four)
        for member in range(LEAF_DEV):
            bits = masks[member] >> (4 * spot)
            table[T_FAR + 8 * index + 2 * member] = (bits >> first) & 1
            table[T_FAR + 8 * index + 2 * member + 1] = jnp.where(first == second, 0, (bits >> second) & 1)


def add_tile(left, right, samples, total, member):
    start = pl.multiple_of(member * LEAF_PTS, LEAF_PTS)
    exponent = jnp.dot(left[pl.ds(start, LEAF_PTS), :], right, preferred_element_type=F32)
    tile = jnp.exp(exponent).astype(BF16)
    total[member] += jnp.dot(tile, samples, preferred_element_type=F32)


def own_kernel(table, points, omega, total, left):
    for member in range(LEAF_DEV):
        coords = points[:, member * LEAF_PTS:(member + 1) * LEAF_PTS]
        left[member * LEAF_PTS:(member + 1) * LEAF_PTS, :] = left_side(coords.astype(F32)).astype(F32).T.astype(BF16)
    total[...] = jnp.zeros_like(total)

    def source_step(source, carry):
        coords = points[:, pl.ds(pl.multiple_of(source * LEAF_PTS, LEAF_PTS), LEAF_PTS)]
        right = right_side(coords.astype(F32))
        samples = omega[source]

        def member_step(member, inner):
            @pl.when(table[T_OWN + LEAF_DEV * member + source] > 0)
            def _():
                add_tile(left, right, samples, total, member)
            return inner

        return lax.fori_loop(0, LEAF_DEV, member_step, carry)

    lax.fori_loop(0, LEAF_DEV, source_step, 0)


def add_packs(group, table, left, packs, total):
    for index, pack in zip(group, packs):

        def slot_step(slot, carry, index=index, pack=pack):
            pieces = [pack[slot, LEAF_PTS + DIMS * c:LEAF_PTS + DIMS * (c + 1), :] for c in range(LEAF_PTS // 128)]
            coords = jnp.concatenate([p.astype(F32) for p in pieces], axis=1)
            right = right_side(coords)
            samples = pack[slot, 0:LEAF_PTS, :]

            def member_step(member, inner):
                @pl.when(table[T_FAR + 8 * index + 2 * member + slot] > 0)
                def _():
                    add_tile(left, right, samples, total, member)
                return inner

            return lax.fori_loop(0, LEAF_DEV, member_step, carry)

        lax.fori_loop(0, SLOTS, slot_step, 0)


def early_kernel(group, table, left, points, pivots, before, *rest):
    packs, (total, skeleton) = rest[:len(group)], rest[len(group):]
    total[...] = before[...]
    for member in range(LEAF_DEV):
        coords = points[:, member * LEAF_PTS:(member + 1) * LEAF_PTS]
        chosen = lax.broadcasted_iota(jnp.int32, (LEAF_PTS, SKEL), 0) == pivots[member:member + 1, :]
        picked = jnp.dot(coords, jnp.where(chosen, 1.0, 0.0).astype(BF16), preferred_element_type=F32)
        skeleton[:, member * SKEL:(member + 1) * SKEL] = picked.astype(BF16)
    add_packs(group, table, left, packs, total)


def late_kernel(group, table, left, before, *rest):
    packs, (total, *blocks) = rest[:len(group)], rest[len(group):]
    total[...] = before[...]
    add_packs(group, table, left, packs, total)
    column = lax.axis_index("samp")
    for step in range(4):
        blocks[step][...] = total[(column + step) & 3].astype(BF16)


def rows_kernel(total, pivots, skeleton, sibling, rows, coupling):
    for member in range(LEAF_DEV):
        chosen = lax.broadcasted_iota(jnp.int32, (LEAF_PTS, SKEL), 0) == pivots[member:member + 1, :]
        pick = jnp.where(chosen, 1.0, 0.0)
        values = total[member]
        rows[member * SKEL:(member + 1) * SKEL, :] = lax.dot_general(pick, values, (((0,), (0,)), ((), ())), preferred_element_type=F32, precision=HIGHEST)
    exponent = dot_tn(left_side(skeleton[...].astype(F32)), right_side(sibling[...].astype(F32)))
    coupling[...] = jnp.exp(exponent).astype(BF16)


def matmul3(a, b):
    a_high = a.astype(BF16)
    a_low = (a - a_high.astype(F32)).astype(BF16)
    b_high = b.astype(BF16)
    b_low = (b - b_high.astype(F32)).astype(BF16)
    dot = functools.partial(jnp.dot, preferred_element_type=F32)
    return dot(a_high, b_high) + (dot(a_high, b_low) + dot(a_low, b_high))


def inverse(gram):
    row = lax.broadcasted_iota(jnp.int32, (SKEL, SKEL), 0)
    eye = jnp.where(row == lax.broadcasted_iota(jnp.int32, (SKEL, SKEL), 1), 1.0, 0.0)
    trace = jnp.sum(jnp.sum(gram * eye, axis=1, keepdims=True), axis=0, keepdims=True)
    shift = RIDGE * trace / SKEL
    scaled = gram / shift + eye
    spread = 1.0 + SKEL / RIDGE
    error = (spread - 1.0) / (spread + 1.0)
    start = 2.0 / (1.0 + spread)
    guess = start * (2.0 * eye - start * scaled)
    error = error * error
    steps = 0
    while error > 1e-9:
        factor = 2.0 / (2.0 - error)
        guess = guess * factor
        error = error / (2.0 - error)
        late = error < 0.1
        multiply = functools.partial(jnp.dot, precision=HIGHEST, preferred_element_type=F32) if late else matmul3
        guess = 2.0 * guess - multiply(guess, multiply(scaled, guess))
        error = error * error
        steps += 1
    return guess / shift


def solve_kernel(b0, b1, b2, b3, pivots, rows, coupling, interpolation):
    del rows, coupling
    column = lax.axis_index("samp")
    mine = pivots[pl.ds(column, 1), :]
    chosen = lax.broadcasted_iota(jnp.int32, (LEAF_PTS, SKEL), 0) == mine
    pick = jnp.where(chosen, 1.0, 0.0).astype(BF16)
    gram = jnp.zeros((SKEL, SKEL), F32)
    cross = jnp.zeros((LEAF_PTS, SKEL), F32)
    for block in (b0, b1, b2, b3):
        values = block[...]
        rows = dot_tn(pick, values).astype(BF16)
        gram += dot_nt(rows, rows)
        cross += dot_nt(values, rows)
    interpolation[...] = jnp.dot(cross, inverse(gram), precision=HIGHEST, preferred_element_type=F32).astype(BF16)


def project_kernel(i0, i1, i2, i3, omega, projected):
    column = lax.axis_index("samp")
    for step, block in enumerate((i0, i1, i2, i3)):
        leaf = (column - step) & 3
        spot = pl.ds(pl.multiple_of(leaf * SKEL, SKEL), SKEL)
        projected[spot, :] = dot_tn(block[...], omega[leaf]).astype(BF16)


def stack_kernel(i0, i1, i2, i3, interpolation):
    column = lax.axis_index("samp")
    for step, block in enumerate((i0, i1, i2, i3)):
        leaf = (column - step) & 3
        interpolation[pl.ds(pl.multiple_of(leaf * LEAF_PTS, LEAF_PTS), LEAF_PTS), :] = block[...]


def parent_kernel(rows, coupling, projected, parent):
    parent[...] = rows[...] - jnp.dot(coupling[...], projected[...], preferred_element_type=F32)


def general_sample(points, omega, near_lists, leaf_order):
    nodes = lax.axis_size("leaf")
    me = lax.axis_index("leaf")
    columns = omega.shape[1]
    references = LEAF_DEV * NEAR
    tree = jnp.take(leaf_order, near_lists, axis=0).reshape(nodes, references)
    leaf = lax.broadcasted_iota(jnp.int32, (1, 1, LEAF_DEV), 2)
    wants = jnp.any(tree[:, :, None] == me * LEAF_DEV + leaf, axis=1)
    first = jnp.argmax(wants, axis=1).astype(jnp.int32)
    second = (LEAF_DEV - 1 - jnp.argmax(wants[:, ::-1], axis=1)).astype(jnp.int32)
    send = jnp.stack([first, second], axis=1).reshape(-1)
    leaf_points = jnp.moveaxis(points.reshape(DIMS, LEAF_DEV, LEAF_PTS), 1, 0)
    got_points = lax.all_to_all(jnp.take(leaf_points, send, axis=0), "leaf", 0, 0, tiled=True)
    got_samples = lax.all_to_all(jnp.take(omega.reshape(LEAF_DEV, LEAF_PTS, columns), send, axis=0), "leaf", 0, 0, tiled=True)
    mine = lax.dynamic_index_in_dim(tree, me, 0, keepdims=False)
    smaller = jnp.any(jnp.logical_and((mine[:, None] >> 2) == (mine[None, :] >> 2), mine[None, :] < mine[:, None]), axis=1)
    arrival = ((mine >> 2) * SLOTS + smaller.astype(jnp.int32)).reshape(LEAF_DEV, NEAR)

    def one(member):
        slots = lax.dynamic_index_in_dim(arrival, member, 0, keepdims=False)
        far = jnp.moveaxis(jnp.take(got_points, slots, axis=0), 0, 1).reshape(DIMS, NEAR * LEAF_PTS)
        samples = jnp.take(got_samples, slots, axis=0).reshape(NEAR * LEAF_PTS, columns)
        own = lax.dynamic_index_in_dim(leaf_points, member, 0, keepdims=False)
        own_f, far_f = own.astype(F32), far.astype(F32)
        inner = jnp.dot(own.T, far, preferred_element_type=F32)
        distance = jnp.sum(own_f * own_f, 0)[:, None] + jnp.sum(far_f * far_f, 0)[None, :] - 2.0 * inner
        return jnp.dot(jnp.exp(-RATE * distance).astype(BF16), samples, preferred_element_type=F32)

    return lax.map(one, jnp.arange(LEAF_DEV, dtype=jnp.int32))


def call(kernel, name, out_shape, in_specs, out_specs, **more):
    return pl.pallas_call(
        kernel,
        name=name,
        out_shape=out_shape,
        in_specs=in_specs,
        out_specs=out_specs,
        compiler_params=pltpu.CompilerParams(vmem_limit_bytes=VMEM_LIMIT),
        **more,
    )


def shards(points, omega, near_lists, leaf_order, pivots):
    columns = omega.shape[1]
    near = near_lists.T
    leaves = omega.reshape(LEAF_DEV, LEAF_PTS, columns)
    shape = jax.ShapeDtypeStruct
    block = shape((LEAF_PTS, columns), BF16)
    smem = pl.BlockSpec(memory_space=SMEM)
    anywhere = pl.BlockSpec(memory_space=pl.ANY)
    table, *packs = call(
        send_kernel,
        "send",
        [shape((T_LEN,), jnp.int32)] + [shape((SLOTS, PACK, columns), BF16)] * CLASSES,
        [smem, smem] + vm(3),
        [smem] + vm(CLASSES),
    )(near, leaf_order, near, points, leaves)

    total_shape = shape((LEAF_DEV, LEAF_PTS, columns), F32)

    def shift(value, k):
        return lax.ppermute(value, "samp", [(s, (s + k) % 4) for s in range(4)])

    def near_branch(points, leaves, near_lists, leaf_order, pivots, table, packs):
        arrived = [
            lax.ppermute(pack, "leaf", [((n + offset) % NODES, n) for n in range(NODES)])
            for pack, offset in zip(packs, OFFSETS)
        ]
        total, left = call(
            own_kernel, "own", [total_shape, shape((LEAF_DEV * LEAF_PTS, AUG), BF16)], [smem] + vm(2), vm(2)
        )(table, points, leaves)
        total, skeleton = call(
            functools.partial(early_kernel, EARLY),
            "early",
            [total_shape, shape((DIMS, LEAF_DEV * SKEL), BF16)],
            [smem] + vm(4 + len(EARLY)),
            vm(2),
        )(table, left, points, pivots, total, *[arrived[i] for i in EARLY])
        sibling = lax.ppermute(skeleton, "leaf", [(n, n ^ 1) for n in range(NODES)])
        total, *blocks = call(
            functools.partial(late_kernel, LATE), "late", [total_shape] + [block] * 4, [smem] + vm(2 + len(LATE)), vm(5)
        )(table, left, total, *[arrived[i] for i in LATE])
        return total, blocks, skeleton, sibling

    def any_branch(points, leaves, near_lists, leaf_order, pivots, table, packs):
        total = general_sample(points, leaves.reshape(-1, columns), near_lists, leaf_order)
        column = lax.axis_index("samp")
        blocks = [lax.dynamic_index_in_dim(total, (column + k) & 3, 0, keepdims=False).astype(BF16) for k in range(4)]
        leaf_points = points.reshape(DIMS, LEAF_DEV, LEAF_PTS)
        skeleton = jnp.take_along_axis(leaf_points, pivots[None], axis=2).reshape(DIMS, LEAF_DEV * SKEL)
        return total, blocks, skeleton, lax.ppermute(skeleton, "leaf", [(n, n ^ 1) for n in range(NODES)])

    total, blocks, skeleton, sibling = lax.cond(
        table[T_OK] > 0, near_branch, any_branch, points, leaves, near_lists, leaf_order, pivots, table, packs
    )
    swapped = [blocks[0]] + [shift(blocks[k], k) for k in range(1, 4)]
    rows, coupling = call(
        rows_kernel,
        "rows",
        [shape((LEAF_DEV * SKEL, columns), F32), shape((LEAF_DEV * SKEL, LEAF_DEV * SKEL), BF16)],
        vm(4),
        vm(2),
    )(total, pivots, skeleton, sibling)
    (interpolation,) = call(
        solve_kernel, "solve", [shape((LEAF_PTS, SKEL), BF16)], vm(5) + [anywhere] * 2, vm(1)
    )(*swapped, pivots, rows, coupling)
    spread = [interpolation] + [shift(interpolation, k) for k in range(1, 4)]
    (projected,) = call(project_kernel, "project", [shape((LEAF_DEV * SKEL, columns), BF16)], vm(5), vm(1))(*spread, leaves)
    crossed = lax.ppermute(projected, "leaf", [(n, n ^ 1) for n in range(NODES)])
    (stacked,) = call(stack_kernel, "stack", [shape((LEAF_DEV * LEAF_PTS, SKEL), BF16)], vm(4), vm(1))(*spread)
    (parent,) = call(parent_kernel, "parent", [shape((LEAF_DEV * SKEL, columns), F32)], vm(3), vm(1))(rows, coupling, crossed)
    return stacked, parent


def solution(mesh):
    placed = (P(None, "leaf"), P("leaf", "samp"), P(), P(), P("leaf", None))
    return jax.shard_map(
        shards,
        mesh=mesh,
        in_specs=placed,
        out_specs=(P("leaf", None), P("leaf", "samp")),
        check_vma=False,
    )
```

```python
import functools

import jax
import jax.numpy as jnp
from jax import lax
from jax.experimental import pallas as pl
from jax.experimental.pallas import tpu as pltpu
from jax.sharding import PartitionSpec as P

DIMS = 8
LEAF_PTS = 512
NEAR = 8
SKEL = 128
SLOTS = 2
LEAF_DEV = 4
REACH = 3
LEAVES = 256
NODES = LEAVES // LEAF_DEV
RIDGE = 0.1
RATE = 0.25

AUG = 16
PACK = LEAF_PTS + DIMS * LEAF_PTS // 128
SIBLING, BEHIND, BEHIND_ACROSS, AHEAD, MIXED, FAR = (1, -1), (-2, -2), (-1, -3), (2, 2), (-3, 1), (NODES // 2, NODES // 2)
OFFSETS = (BEHIND, BEHIND_ACROSS, AHEAD, MIXED, SIBLING, FAR)
CLASSES = len(OFFSETS)
HALF = CLASSES - 1
GROUPS = ((4, 0, 1), (2, 3), (HALF,))
AFTER = (0,)
T_HALF = 96
T_OK = 0
T_OWN = 8
T_FAR = 32
T_LEN = 128
VMEM_LIMIT = 16 << 20

VMEM = pltpu.VMEM
SMEM = pltpu.SMEM
F32 = jnp.float32
BF16 = jnp.bfloat16
HIGHEST = lax.Precision.HIGHEST


def vm(count):
    return [pl.BlockSpec(memory_space=VMEM)] * count


def dot_tn(a, b):
    return lax.dot_general(a, b, (((0,), (0,)), ((), ())), preferred_element_type=F32)


def dot_nt(a, b):
    return lax.dot_general(a, b, (((1,), (1,)), ((), ())), preferred_element_type=F32)


def split_norm(coords):
    norm = RATE * jnp.sum(coords * coords, axis=0, keepdims=True)
    high = norm.astype(BF16).astype(F32)
    rest = norm - high
    middle = rest.astype(BF16).astype(F32)
    low = rest - middle
    return high, middle, low


def left_side(coords):
    high, middle, low = split_norm(coords)
    row = lax.broadcasted_iota(jnp.int32, (DIMS, coords.shape[1]), 0)
    extra = jnp.where(row == 0, -high, jnp.where(row == 1, -middle, jnp.where(row == 2, -low, jnp.where(row < 6, 1.0, 0.0))))
    return jnp.concatenate([coords * (2.0 * RATE), extra], axis=0).astype(BF16)


def right_side(coords):
    high, middle, low = split_norm(coords)
    row = lax.broadcasted_iota(jnp.int32, (DIMS, coords.shape[1]), 0)
    extra = jnp.where(row == 3, -high, jnp.where(row == 4, -middle, jnp.where(row == 5, -low, jnp.where(row < 3, 1.0, 0.0))))
    return jnp.concatenate([coords, extra], axis=0).astype(BF16)


def fill_pack(pack, leaves, points, omega):
    for slot, leaf in enumerate(leaves):
        pack[slot, 0:LEAF_PTS, :] = omega[leaf]
        mine = points[:, pl.ds(pl.multiple_of(leaf * LEAF_PTS, LEAF_PTS), LEAF_PTS)]
        for piece in range(LEAF_PTS // 128):
            pack[slot, LEAF_PTS + DIMS * piece:LEAF_PTS + DIMS * (piece + 1), :] = mine[:, 128 * piece:128 * (piece + 1)]


def send_kernel(near_s, order_s, near_v, points, omega, table, *packs):
    me = lax.axis_index("leaf")
    near = near_v[...]

    def look(k, tree):
        return jnp.where(near == k, order_s[k], tree)

    tree = lax.fori_loop(0, LEAVES, look, jnp.zeros((NEAR, LEAVES), jnp.int32), unroll=16)
    node = lax.broadcasted_iota(jnp.int32, (NEAR, LEAVES), 1) >> 2
    part = tree & 3
    weight = jnp.where(part == 0, 1.0, jnp.where(part == 1, 8.0, jnp.where(part == 2, 64.0, 512.0)))
    weight = jnp.where((tree >> 2) == me, weight, 0.0)
    for index, offset in enumerate(OFFSETS):
        even, odd = offset
        requester = (me - jnp.where((me ^ even) & 1 > 0, odd, even)) & (NODES - 1)
        counts = jnp.sum(jnp.where(node == requester, weight, 0.0)).astype(jnp.int32)
        has = [(counts >> (3 * leaf)) & 7 > 0 for leaf in range(LEAF_DEV)]
        first = jnp.where(has[0], 0, jnp.where(has[1], 1, jnp.where(has[2], 2, jnp.where(has[3], 3, 0))))
        second = jnp.where(has[3], 3, jnp.where(has[2], 2, jnp.where(has[1], 1, 0)))
        if index == HALF:
            table[T_HALF], table[T_HALF + 1] = first, second
        else:
            fill_pack(packs[index], (first, second), points, omega)

    place = ((tree >> 2) - node + REACH) & (NODES - 1)
    bad = jnp.logical_and(place >= 2 * REACH, place != REACH + NODES // 2)
    table[T_OK] = jnp.where(jnp.max(jnp.where(bad, 1.0, 0.0)) > 0.0, 0, 1)

    def lowest(mask):
        return jnp.where(mask & 1 > 0, 0, jnp.where(mask & 2 > 0, 1, jnp.where(mask & 4 > 0, 2, jnp.where(mask & 8 > 0, 3, 0))))

    def highest(mask):
        return jnp.where(mask & 8 > 0, 3, jnp.where(mask & 4 > 0, 2, jnp.where(mask & 2 > 0, 1, 0)))

    masks = []
    for member in range(LEAF_DEV):
        mask = jnp.int32(0)
        for entry in range(NEAR):
            leaf = order_s[near_s[entry, me * LEAF_DEV + member]]
            spot = ((leaf >> 2) - me + REACH) & (NODES - 1)
            spot = jnp.where(spot < 2 * REACH, spot, 2 * REACH)
            mask = mask | (jnp.int32(1) << (4 * spot + (leaf & 3)))
        masks.append(mask)
    every = masks[0] | masks[1] | masks[2] | masks[3]
    for member in range(LEAF_DEV):
        for source in range(LEAF_DEV):
            table[T_OWN + LEAF_DEV * member + source] = (masks[member] >> (4 * REACH + source)) & 1
    for index, offset in enumerate(OFFSETS):
        spot = 2 * REACH if index == HALF else jnp.where(me & 1 > 0, offset[1], offset[0]) + REACH
        four = (every >> (4 * spot)) & 15
        first, second = lowest(four), highest(four)
        for member in range(LEAF_DEV):
            bits = masks[member] >> (4 * spot)
            table[T_FAR + 8 * index + 2 * member] = (bits >> first) & 1
            table[T_FAR + 8 * index + 2 * member + 1] = jnp.where(first == second, 0, (bits >> second) & 1)


def add_tile(left, right, samples, total, member):
    start = pl.multiple_of(member * LEAF_PTS, LEAF_PTS)
    exponent = jnp.dot(left[pl.ds(start, LEAF_PTS), :], right, preferred_element_type=F32)
    tile = jnp.exp(exponent).astype(BF16)
    total[member] += jnp.dot(tile, samples, preferred_element_type=F32)


def half_kernel(table, points, omega, *rest):
    fill_pack(rest[-1], (table[T_HALF], table[T_HALF + 1]), points, omega)


def own_kernel(table, points, omega, total, left):
    for member in range(LEAF_DEV):
        coords = points[:, member * LEAF_PTS:(member + 1) * LEAF_PTS]
        left[member * LEAF_PTS:(member + 1) * LEAF_PTS, :] = left_side(coords.astype(F32)).astype(F32).T.astype(BF16)
    total[...] = jnp.zeros_like(total)

    def source_step(source, carry):
        coords = points[:, pl.ds(pl.multiple_of(source * LEAF_PTS, LEAF_PTS), LEAF_PTS)]
        right = right_side(coords.astype(F32))
        samples = omega[source]

        def member_step(member, inner):
            @pl.when(table[T_OWN + LEAF_DEV * member + source] > 0)
            def _():
                add_tile(left, right, samples, total, member)
            return inner

        return lax.fori_loop(0, LEAF_DEV, member_step, carry)

    lax.fori_loop(0, LEAF_DEV, source_step, 0)


def add_packs(group, table, left, packs, total):
    for index, pack in zip(group, packs):

        def slot_step(slot, carry, index=index, pack=pack):
            pieces = [pack[slot, LEAF_PTS + DIMS * c:LEAF_PTS + DIMS * (c + 1), :] for c in range(LEAF_PTS // 128)]
            coords = jnp.concatenate([p.astype(F32) for p in pieces], axis=1)
            right = right_side(coords)
            samples = pack[slot, 0:LEAF_PTS, :]

            def member_step(member, inner):
                @pl.when(table[T_FAR + 8 * index + 2 * member + slot] > 0)
                def _():
                    add_tile(left, right, samples, total, member)
                return inner

            return lax.fori_loop(0, LEAF_DEV, member_step, carry)

        lax.fori_loop(0, SLOTS, slot_step, 0)


def early_kernel(group, table, left, before, *rest):
    packs, (total,) = rest[:len(group)], rest[len(group):]
    total[...] = before[...]
    add_packs(group, table, left, packs, total)


def late_kernel(group, table, left, points, pivots, before, *rest):
    packs, (total, skeleton, *blocks) = rest[:len(group)], rest[len(group):]
    total[...] = before[...]
    add_packs(group, table, left, packs, total)
    column = lax.axis_index("samp")
    for step in range(4):
        blocks[step][...] = total[(column + step) & 3].astype(BF16)
    for member in range(LEAF_DEV):
        coords = points[:, member * LEAF_PTS:(member + 1) * LEAF_PTS]
        chosen = lax.broadcasted_iota(jnp.int32, (LEAF_PTS, SKEL), 0) == pivots[member:member + 1, :]
        picked = jnp.dot(coords, jnp.where(chosen, 1.0, 0.0).astype(BF16), preferred_element_type=F32)
        skeleton[:, member * SKEL:(member + 1) * SKEL] = picked.astype(BF16)


def rows_kernel(total, pivots, skeleton, sibling, rows, coupling):
    for member in range(LEAF_DEV):
        chosen = lax.broadcasted_iota(jnp.int32, (LEAF_PTS, SKEL), 0) == pivots[member:member + 1, :]
        pick = jnp.where(chosen, 1.0, 0.0)
        values = total[member]
        rows[member * SKEL:(member + 1) * SKEL, :] = lax.dot_general(pick, values, (((0,), (0,)), ((), ())), preferred_element_type=F32, precision=HIGHEST)
    exponent = dot_tn(left_side(skeleton[...].astype(F32)), right_side(sibling[...].astype(F32)))
    coupling[...] = jnp.exp(exponent).astype(BF16)


def matmul3(a, b):
    a_high = a.astype(BF16)
    a_low = (a - a_high.astype(F32)).astype(BF16)
    b_high = b.astype(BF16)
    b_low = (b - b_high.astype(F32)).astype(BF16)
    dot = functools.partial(jnp.dot, preferred_element_type=F32)
    return dot(a_high, b_high) + (dot(a_high, b_low) + dot(a_low, b_high))


def inverse(gram):
    row = lax.broadcasted_iota(jnp.int32, (SKEL, SKEL), 0)
    eye = jnp.where(row == lax.broadcasted_iota(jnp.int32, (SKEL, SKEL), 1), 1.0, 0.0)
    trace = jnp.sum(jnp.sum(gram * eye, axis=1, keepdims=True), axis=0, keepdims=True)
    shift = RIDGE * trace / SKEL
    scaled = gram / shift + eye
    spread = 1.0 + SKEL / RIDGE
    error = (spread - 1.0) / (spread + 1.0)
    start = 2.0 / (1.0 + spread)
    guess = start * (2.0 * eye - start * scaled)
    error = error * error
    steps = 0
    while error > 1e-5:
        factor = 2.0 / (2.0 - error)
        guess = guess * factor
        error = error / (2.0 - error)
        late = error < 0.1
        multiply = functools.partial(jnp.dot, precision=HIGHEST, preferred_element_type=F32) if late else matmul3
        guess = 2.0 * guess - multiply(guess, multiply(scaled, guess))
        error = error * error
        steps += 1
    return guess / shift


def solve_kernel(b0, b1, b2, b3, pivots, rows, coupling, interpolation):
    del rows, coupling
    column = lax.axis_index("samp")
    mine = pivots[pl.ds(column, 1), :]
    chosen = lax.broadcasted_iota(jnp.int32, (LEAF_PTS, SKEL), 0) == mine
    pick = jnp.where(chosen, 1.0, 0.0).astype(BF16)
    gram = jnp.zeros((SKEL, SKEL), F32)
    cross = jnp.zeros((LEAF_PTS, SKEL), F32)
    for block in (b0, b1, b2, b3):
        values = block[...]
        rows = dot_tn(pick, values).astype(BF16)
        gram += dot_nt(rows, rows)
        cross += dot_nt(values, rows)
    interpolation[...] = jnp.dot(cross, inverse(gram), precision=HIGHEST, preferred_element_type=F32).astype(BF16)


def project_kernel(i0, i1, i2, i3, omega, projected):
    column = lax.axis_index("samp")
    for step, block in enumerate((i0, i1, i2, i3)):
        leaf = (column - step) & 3
        spot = pl.ds(pl.multiple_of(leaf * SKEL, SKEL), SKEL)
        projected[spot, :] = dot_tn(block[...], omega[leaf]).astype(BF16)


def stack_kernel(i0, i1, i2, i3, interpolation):
    column = lax.axis_index("samp")
    for step, block in enumerate((i0, i1, i2, i3)):
        leaf = (column - step) & 3
        interpolation[pl.ds(pl.multiple_of(leaf * LEAF_PTS, LEAF_PTS), LEAF_PTS), :] = block[...]


def parent_kernel(rows, coupling, projected, parent):
    parent[...] = rows[...] - jnp.dot(coupling[...], projected[...], preferred_element_type=F32)


def general_sample(points, omega, near_lists, leaf_order):
    nodes = lax.axis_size("leaf")
    me = lax.axis_index("leaf")
    columns = omega.shape[1]
    references = LEAF_DEV * NEAR
    tree = jnp.take(leaf_order, near_lists, axis=0).reshape(nodes, references)
    leaf = lax.broadcasted_iota(jnp.int32, (1, 1, LEAF_DEV), 2)
    wants = jnp.any(tree[:, :, None] == me * LEAF_DEV + leaf, axis=1)
    first = jnp.argmax(wants, axis=1).astype(jnp.int32)
    second = (LEAF_DEV - 1 - jnp.argmax(wants[:, ::-1], axis=1)).astype(jnp.int32)
    send = jnp.stack([first, second], axis=1).reshape(-1)
    leaf_points = jnp.moveaxis(points.reshape(DIMS, LEAF_DEV, LEAF_PTS), 1, 0)
    got_points = lax.all_to_all(jnp.take(leaf_points, send, axis=0), "leaf", 0, 0, tiled=True)
    got_samples = lax.all_to_all(jnp.take(omega.reshape(LEAF_DEV, LEAF_PTS, columns), send, axis=0), "leaf", 0, 0, tiled=True)
    mine = lax.dynamic_index_in_dim(tree, me, 0, keepdims=False)
    smaller = jnp.any(jnp.logical_and((mine[:, None] >> 2) == (mine[None, :] >> 2), mine[None, :] < mine[:, None]), axis=1)
    arrival = ((mine >> 2) * SLOTS + smaller.astype(jnp.int32)).reshape(LEAF_DEV, NEAR)

    def one(member):
        slots = lax.dynamic_index_in_dim(arrival, member, 0, keepdims=False)
        far = jnp.moveaxis(jnp.take(got_points, slots, axis=0), 0, 1).reshape(DIMS, NEAR * LEAF_PTS)
        samples = jnp.take(got_samples, slots, axis=0).reshape(NEAR * LEAF_PTS, columns)
        own = lax.dynamic_index_in_dim(leaf_points, member, 0, keepdims=False)
        own_f, far_f = own.astype(F32), far.astype(F32)
        inner = jnp.dot(own.T, far, preferred_element_type=F32)
        distance = jnp.sum(own_f * own_f, 0)[:, None] + jnp.sum(far_f * far_f, 0)[None, :] - 2.0 * inner
        return jnp.dot(jnp.exp(-RATE * distance).astype(BF16), samples, preferred_element_type=F32)

    return lax.map(one, jnp.arange(LEAF_DEV, dtype=jnp.int32))


def call(kernel, name, out_shape, in_specs, out_specs, **more):
    return pl.pallas_call(
        kernel,
        name=name,
        out_shape=out_shape,
        in_specs=in_specs,
        out_specs=out_specs,
        compiler_params=pltpu.CompilerParams(vmem_limit_bytes=VMEM_LIMIT),
        **more,
    )


def shards(points, omega, near_lists, leaf_order, pivots):
    columns = omega.shape[1]
    near = near_lists.T
    leaves = omega.reshape(LEAF_DEV, LEAF_PTS, columns)
    shape = jax.ShapeDtypeStruct
    block = shape((LEAF_PTS, columns), BF16)
    smem = pl.BlockSpec(memory_space=SMEM)
    anywhere = pl.BlockSpec(memory_space=pl.ANY)
    pack_shape = shape((SLOTS, PACK, columns), BF16)
    table, *packs = call(
        send_kernel,
        "send",
        [shape((T_LEN,), jnp.int32)] + [pack_shape] * HALF,
        [smem, smem] + vm(3),
        [smem] + vm(HALF),
    )(near, leaf_order, near, points, leaves)

    total_shape = shape((LEAF_DEV, LEAF_PTS, columns), F32)

    def shift(value, k):
        return lax.ppermute(value, "samp", [(s, (s + k) % 4) for s in range(4)])

    def near_branch(points, leaves, near_lists, leaf_order, pivots, table, packs):
        def move(pack, offset):
            return lax.ppermute(pack, "leaf", [((n + offset[n % 2]) % NODES, n) for n in range(NODES)])

        arrived = [move(packs[i], OFFSETS[i]) for i in range(HALF)]
        total, left = call(
            own_kernel, "own", [total_shape, shape((LEAF_DEV * LEAF_PTS, AUG), BF16)], [smem] + vm(2), vm(2)
        )(table, points, leaves)
        (half,) = call(half_kernel, "half", [pack_shape], [smem] + vm(2) + [anywhere] * (1 + len(AFTER)), vm(1))(
            table, points, leaves, left, *[arrived[i] for i in AFTER]
        )
        arrived.append(move(half, OFFSETS[HALF]))
        for step, group in enumerate(GROUPS[:-1]):
            (total,) = call(
                functools.partial(early_kernel, group), f"early{step}", [total_shape], [smem] + vm(2 + len(group)), vm(1)
            )(table, left, total, *[arrived[i] for i in group])
        total, skeleton, *blocks = call(
            functools.partial(late_kernel, GROUPS[-1]),
            "late",
            [total_shape, shape((DIMS, LEAF_DEV * SKEL), BF16)] + [block] * 4,
            [smem] + vm(4 + len(GROUPS[-1])),
            vm(6),
        )(table, left, points, pivots, total, *[arrived[i] for i in GROUPS[-1]])
        return total, blocks, skeleton

    def any_branch(points, leaves, near_lists, leaf_order, pivots, table, packs):
        total = general_sample(points, leaves.reshape(-1, columns), near_lists, leaf_order)
        column = lax.axis_index("samp")
        blocks = [lax.dynamic_index_in_dim(total, (column + k) & 3, 0, keepdims=False).astype(BF16) for k in range(4)]
        leaf_points = points.reshape(DIMS, LEAF_DEV, LEAF_PTS)
        skeleton = jnp.take_along_axis(leaf_points, pivots[None], axis=2).reshape(DIMS, LEAF_DEV * SKEL)
        return total, blocks, skeleton

    total, blocks, skeleton = lax.cond(
        table[T_OK] > 0, near_branch, any_branch, points, leaves, near_lists, leaf_order, pivots, table, packs
    )
    swapped = [blocks[0]] + [shift(blocks[k], k) for k in range(1, 4)]
    sibling = lax.ppermute(skeleton, "leaf", [(n, n ^ 1) for n in range(NODES)])
    rows, coupling = call(
        rows_kernel,
        "rows",
        [shape((LEAF_DEV * SKEL, columns), F32), shape((LEAF_DEV * SKEL, LEAF_DEV * SKEL), BF16)],
        vm(4),
        vm(2),
    )(total, pivots, skeleton, sibling)
    (interpolation,) = call(
        solve_kernel, "solve", [shape((LEAF_PTS, SKEL), BF16)], vm(5) + [anywhere] * 2, vm(1)
    )(*swapped, pivots, rows, coupling)
    spread = [interpolation] + [shift(interpolation, k) for k in range(1, 4)]
    (projected,) = call(project_kernel, "project", [shape((LEAF_DEV * SKEL, columns), BF16)], vm(5), vm(1))(*spread, leaves)
    crossed = lax.ppermute(projected, "leaf", [(n, n ^ 1) for n in range(NODES)])
    (stacked,) = call(stack_kernel, "stack", [shape((LEAF_DEV * LEAF_PTS, SKEL), BF16)], vm(4), vm(1))(*spread)
    (parent,) = call(parent_kernel, "parent", [shape((LEAF_DEV * SKEL, columns), F32)], vm(3), vm(1))(rows, coupling, crossed)
    return stacked, parent


def solution(mesh):
    placed = (P(None, "leaf"), P("leaf", "samp"), P(), P(), P("leaf", None))
    return jax.shard_map(
        shards,
        mesh=mesh,
        in_specs=placed,
        out_specs=(P("leaf", None), P("leaf", "samp")),
        check_vma=False,
    )
```

```python
import functools

import jax
import jax.numpy as jnp
from jax import lax
from jax.experimental import pallas as pl
from jax.experimental.pallas import tpu as pltpu
from jax.sharding import PartitionSpec as P


DIMS = 8
LEAF_PTS = 512
NEAR = 8
SKEL = 128
SLOTS = 2
LEAF_DEV = 4
REACH = 3
LEAVES = 256
NODES = LEAVES // LEAF_DEV
RIDGE = 0.1
RATE = 0.25

AUG = 16
PACK = LEAF_PTS + DIMS * LEAF_PTS // 128
SIBLING, BEHIND, BEHIND_ACROSS, AHEAD, MIXED, FAR = (1, -1), (-2, -2), (-1, -3), (2, 2), (-3, 1), (NODES // 2, NODES // 2)
OFFSETS = (BEHIND, BEHIND_ACROSS, AHEAD, MIXED, SIBLING, FAR)
CLASSES = len(OFFSETS)
HALF = CLASSES - 1
BESIDE = CLASSES - 2
GROUPS = ((4, 0, 1), (2, 3), (HALF,))
FIRST, SECOND = (0,), (1, 2, 3)
T_LEAF = 96
T_OK = 0
T_OWN = 8
T_FAR = 32
T_LEN = 128
VMEM_LIMIT = 16 << 20

VMEM = pltpu.VMEM
SMEM = pltpu.SMEM
F32 = jnp.float32
BF16 = jnp.bfloat16
HIGHEST = lax.Precision.HIGHEST


def vm(count):
    return [pl.BlockSpec(memory_space=VMEM)] * count


def dot_tn(a, b):
    return lax.dot_general(a, b, (((0,), (0,)), ((), ())), preferred_element_type=F32)


def dot_nt(a, b):
    return lax.dot_general(a, b, (((1,), (1,)), ((), ())), preferred_element_type=F32)


def split_norm(coords):
    norm = RATE * jnp.sum(coords * coords, axis=0, keepdims=True)
    high = norm.astype(BF16).astype(F32)
    rest = norm - high
    middle = rest.astype(BF16).astype(F32)
    low = rest - middle
    return high, middle, low


def left_side(coords):
    high, middle, low = split_norm(coords)
    row = lax.broadcasted_iota(jnp.int32, (DIMS, coords.shape[1]), 0)
    extra = jnp.where(row == 0, -high, jnp.where(row == 1, -middle, jnp.where(row == 2, -low, jnp.where(row < 6, 1.0, 0.0))))
    return jnp.concatenate([coords * (2.0 * RATE), extra], axis=0).astype(BF16)


def right_side(coords):
    high, middle, low = split_norm(coords)
    row = lax.broadcasted_iota(jnp.int32, (DIMS, coords.shape[1]), 0)
    extra = jnp.where(row == 3, -high, jnp.where(row == 4, -middle, jnp.where(row == 5, -low, jnp.where(row < 3, 1.0, 0.0))))
    return jnp.concatenate([coords, extra], axis=0).astype(BF16)


def fill_pack(pack, leaves, points, omega):
    for slot, leaf in enumerate(leaves):
        pack[slot, 0:LEAF_PTS, :] = omega[leaf]
        mine = points[:, pl.ds(pl.multiple_of(leaf * LEAF_PTS, LEAF_PTS), LEAF_PTS)]
        for piece in range(LEAF_PTS // 128):
            pack[slot, LEAF_PTS + DIMS * piece:LEAF_PTS + DIMS * (piece + 1), :] = mine[:, 128 * piece:128 * (piece + 1)]


def send_kernel(near_s, order_s, near_v, order_v, points, omega, table, *packs):
    me = lax.axis_index("leaf")
    halves = [jnp.broadcast_to(order_v[part:part + 1, :], (NEAR, 128)) for part in range(LEAVES // 128)]

    def look(near):
        found = jnp.zeros((NEAR, 128), jnp.int32)
        for part, half in enumerate(halves):
            here = jnp.take_along_axis(half, near & 127, axis=1, mode="promise_in_bounds")
            found = jnp.where(near >> 7 == part, here, found)
        return found

    near = near_v[...]
    tree = jnp.concatenate([look(near[:, 128 * part:128 * (part + 1)]) for part in range(LEAVES // 128)], axis=1)
    node = lax.broadcasted_iota(jnp.int32, (NEAR, LEAVES), 1) >> 2
    part = tree & 3
    weight = jnp.where(part == 0, 1.0, jnp.where(part == 1, 8.0, jnp.where(part == 2, 64.0, 512.0)))
    weight = jnp.where((tree >> 2) == me, weight, 0.0)
    for index, offset in enumerate(OFFSETS):
        even, odd = offset
        requester = (me - jnp.where((me ^ even) & 1 > 0, odd, even)) & (NODES - 1)
        counts = jnp.sum(jnp.where(node == requester, weight, 0.0)).astype(jnp.int32)
        has = [(counts >> (3 * leaf)) & 7 > 0 for leaf in range(LEAF_DEV)]
        first = jnp.where(has[0], 0, jnp.where(has[1], 1, jnp.where(has[2], 2, jnp.where(has[3], 3, 0))))
        second = jnp.where(has[3], 3, jnp.where(has[2], 2, jnp.where(has[1], 1, 0)))
        if index >= BESIDE:
            table[T_LEAF + 2 * index], table[T_LEAF + 2 * index + 1] = first, second
        else:
            fill_pack(packs[index], (first, second), points, omega)

    place = ((tree >> 2) - node + REACH) & (NODES - 1)
    bad = jnp.logical_and(place >= 2 * REACH, place != REACH + NODES // 2)
    table[T_OK] = jnp.where(jnp.max(jnp.where(bad, 1.0, 0.0)) > 0.0, 0, 1)

    def lowest(mask):
        return jnp.where(mask & 1 > 0, 0, jnp.where(mask & 2 > 0, 1, jnp.where(mask & 4 > 0, 2, jnp.where(mask & 8 > 0, 3, 0))))

    def highest(mask):
        return jnp.where(mask & 8 > 0, 3, jnp.where(mask & 4 > 0, 2, jnp.where(mask & 2 > 0, 1, 0)))

    masks = []
    for member in range(LEAF_DEV):
        mask = jnp.int32(0)
        for entry in range(NEAR):
            leaf = order_s[near_s[entry, me * LEAF_DEV + member]]
            spot = ((leaf >> 2) - me + REACH) & (NODES - 1)
            spot = jnp.where(spot < 2 * REACH, spot, 2 * REACH)
            mask = mask | (jnp.int32(1) << (4 * spot + (leaf & 3)))
        masks.append(mask)
    every = masks[0] | masks[1] | masks[2] | masks[3]
    for member in range(LEAF_DEV):
        for source in range(LEAF_DEV):
            table[T_OWN + LEAF_DEV * member + source] = (masks[member] >> (4 * REACH + source)) & 1
    for index, offset in enumerate(OFFSETS):
        spot = 2 * REACH if index == HALF else jnp.where(me & 1 > 0, offset[1], offset[0]) + REACH
        four = (every >> (4 * spot)) & 15
        first, second = lowest(four), highest(four)
        for member in range(LEAF_DEV):
            bits = masks[member] >> (4 * spot)
            table[T_FAR + 8 * index + 2 * member] = (bits >> first) & 1
            table[T_FAR + 8 * index + 2 * member + 1] = jnp.where(first == second, 0, (bits >> second) & 1)


def add_tile(left, right, samples, total, member):
    start = pl.multiple_of(member * LEAF_PTS, LEAF_PTS)
    exponent = jnp.dot(left[pl.ds(start, LEAF_PTS), :], right, preferred_element_type=F32)
    tile = jnp.exp(exponent).astype(BF16)
    total[member] += jnp.dot(tile, samples, preferred_element_type=F32)


def own_kernel(table, points, omega, total, left):
    for member in range(LEAF_DEV):
        coords = points[:, member * LEAF_PTS:(member + 1) * LEAF_PTS]
        left[member * LEAF_PTS:(member + 1) * LEAF_PTS, :] = left_side(coords.astype(F32)).astype(F32).T.astype(BF16)
    total[...] = jnp.zeros_like(total)

    def source_step(source, carry):
        coords = points[:, pl.ds(pl.multiple_of(source * LEAF_PTS, LEAF_PTS), LEAF_PTS)]
        right = right_side(coords.astype(F32))
        samples = omega[source]

        def member_step(member, inner):
            @pl.when(table[T_OWN + LEAF_DEV * member + source] > 0)
            def _():
                add_tile(left, right, samples, total, member)

            return inner

        return lax.fori_loop(0, LEAF_DEV, member_step, carry)

    lax.fori_loop(0, LEAF_DEV, source_step, 0)


def half_kernel(table, points, omega, pivots, left, behind, skeleton, beside, half):
    del left, behind
    for index, pack in ((BESIDE, beside), (HALF, half)):
        fill_pack(pack, (table[T_LEAF + 2 * index], table[T_LEAF + 2 * index + 1]), points, omega)
    for member in range(LEAF_DEV):
        coords = points[:, member * LEAF_PTS:(member + 1) * LEAF_PTS]
        chosen = lax.broadcasted_iota(jnp.int32, (LEAF_PTS, SKEL), 0) == pivots[member:member + 1, :]
        picked = jnp.dot(coords, jnp.where(chosen, 1.0, 0.0).astype(BF16), preferred_element_type=F32).astype(BF16)
        skeleton[:, member * SKEL:(member + 1) * SKEL] = picked
        slot, row = divmod(member, SLOTS)
        beside[slot, PACK + DIMS * row:PACK + DIMS * (row + 1), :] = picked


def add_packs(group, table, left, packs, total):
    for index, pack in zip(group, packs):

        def slot_step(slot, carry, index=index, pack=pack):
            pieces = [pack[slot, LEAF_PTS + DIMS * c:LEAF_PTS + DIMS * (c + 1), :] for c in range(LEAF_PTS // 128)]
            coords = jnp.concatenate([p.astype(F32) for p in pieces], axis=1)
            right = right_side(coords)
            samples = pack[slot, 0:LEAF_PTS, :]

            def member_step(member, inner):
                @pl.when(table[T_FAR + 8 * index + 2 * member + slot] > 0)
                def _():
                    add_tile(left, right, samples, total, member)

                return inner

            return lax.fori_loop(0, LEAF_DEV, member_step, carry)

        lax.fori_loop(0, SLOTS, slot_step, 0)


def early_kernel(group, table, left, before, *rest):
    packs, (total,) = rest[:len(group)], rest[len(group):]
    total[...] = before[...]
    add_packs(group, table, left, packs, total)


def couple_kernel(group, table, left, before, skeleton, beside, *rest):
    packs, (total, coupling) = rest[:len(group)], rest[len(group):]
    early_kernel(group, table, left, before, *packs, total)
    places = [divmod(member, SLOTS) for member in range(LEAF_DEV)]
    pieces = [beside[slot, PACK + DIMS * row:PACK + DIMS * (row + 1), :] for slot, row in places]
    sibling = jnp.concatenate([piece.astype(F32) for piece in pieces], axis=1)
    exponent = dot_tn(left_side(skeleton[...].astype(F32)), right_side(sibling))
    coupling[...] = jnp.exp(exponent).astype(BF16)


def late_kernel(group, table, left, before, *rest):
    packs, (total, *blocks) = rest[:len(group)], rest[len(group):]
    total[...] = before[...]
    add_packs(group, table, left, packs, total)
    column = lax.axis_index("samp")
    for step in range(4):
        blocks[step][...] = total[(column + step) & 3].astype(BF16)


def rows_kernel(total, pivots, rows):
    for member in range(LEAF_DEV):
        chosen = lax.broadcasted_iota(jnp.int32, (LEAF_PTS, SKEL), 0) == pivots[member:member + 1, :]
        pick = jnp.where(chosen, 1.0, 0.0)
        values = total[member]
        rows[member * SKEL:(member + 1) * SKEL, :] = lax.dot_general(pick, values, (((0,), (0,)), ((), ())), preferred_element_type=F32, precision=HIGHEST)


def matmul3(a, b):
    a_high = a.astype(BF16)
    a_low = (a - a_high.astype(F32)).astype(BF16)
    b_high = b.astype(BF16)
    b_low = (b - b_high.astype(F32)).astype(BF16)
    left = jnp.concatenate([a_high, a_high, a_low], axis=1)
    right = jnp.concatenate([b_high, b_low, b_high], axis=0)
    return jnp.dot(left, right, preferred_element_type=F32)


def inverse(gram):
    row = lax.broadcasted_iota(jnp.int32, (SKEL, SKEL), 0)
    eye = jnp.where(row == lax.broadcasted_iota(jnp.int32, (SKEL, SKEL), 1), 1.0, 0.0)
    trace = jnp.sum(jnp.sum(gram * eye, axis=1, keepdims=True), axis=0, keepdims=True)
    shift = RIDGE * trace / SKEL
    scaled = gram / shift + eye
    spread = 1.0 + SKEL / RIDGE
    error = (spread - 1.0) / (spread + 1.0)
    start = 2.0 / (1.0 + spread)
    guess = start * (2.0 * eye - start * scaled)
    error = error * error
    while error > 1e-5:
        factor = 2.0 / (2.0 - error)
        guess = guess * factor
        error = error / (2.0 - error)
        late = error < 0.1
        multiply = functools.partial(jnp.dot, precision=HIGHEST, preferred_element_type=F32) if late else matmul3
        guess = 2.0 * guess - multiply(guess, multiply(scaled, guess))
        error = error * error
    return guess / shift


def solve_kernel(b0, b1, b2, b3, pivots, rows, interpolation):
    del rows
    column = lax.axis_index("samp")
    mine = pivots[pl.ds(column, 1), :]
    chosen = lax.broadcasted_iota(jnp.int32, (LEAF_PTS, SKEL), 0) == mine
    pick = jnp.where(chosen, 1.0, 0.0).astype(BF16)
    gram = jnp.zeros((SKEL, SKEL), F32)
    cross = jnp.zeros((LEAF_PTS, SKEL), F32)
    for block in (b0, b1, b2, b3):
        values = block[...]
        rows = dot_tn(pick, values).astype(BF16)
        gram += dot_nt(rows, rows)
        cross += dot_nt(values, rows)
    interpolation[...] = jnp.dot(cross, inverse(gram), precision=HIGHEST, preferred_element_type=F32).astype(BF16)


def project_kernel(steps, omega, *rest):
    column = lax.axis_index("samp")
    projected = rest[-1]
    if len(rest) > len(steps) + 1:
        projected[...] = rest[0][...]
    for step, block in zip(steps, rest[-1 - len(steps):-1]):
        leaf = (column - step) & 3
        spot = pl.ds(pl.multiple_of(leaf * SKEL, SKEL), SKEL)
        projected[spot, :] = dot_tn(block[...], omega[leaf]).astype(BF16)


def stack_kernel(i0, i1, i2, i3, interpolation):
    column = lax.axis_index("samp")
    for step, block in enumerate((i0, i1, i2, i3)):
        leaf = (column - step) & 3
        interpolation[pl.ds(pl.multiple_of(leaf * LEAF_PTS, LEAF_PTS), LEAF_PTS), :] = block[...]


def parent_kernel(rows, coupling, projected, parent):
    parent[...] = rows[...] - jnp.dot(coupling[...], projected[...], preferred_element_type=F32)


def kernel_tile(own, far):
    own_f, far_f = own.astype(F32), far.astype(F32)
    inner = jnp.dot(own.T, far, preferred_element_type=F32)
    distance = jnp.sum(own_f * own_f, 0)[:, None] + jnp.sum(far_f * far_f, 0)[None, :] - 2.0 * inner
    return jnp.exp(-RATE * distance).astype(BF16)


def general_sample(points, omega, near_lists, leaf_order):
    nodes = lax.axis_size("leaf")
    me = lax.axis_index("leaf")
    columns = omega.shape[1]
    references = LEAF_DEV * NEAR
    tree = jnp.take(leaf_order, near_lists, axis=0).reshape(nodes, references)
    leaf = lax.broadcasted_iota(jnp.int32, (1, 1, LEAF_DEV), 2)
    wants = jnp.any(tree[:, :, None] == me * LEAF_DEV + leaf, axis=1)
    first = jnp.argmax(wants, axis=1).astype(jnp.int32)
    second = (LEAF_DEV - 1 - jnp.argmax(wants[:, ::-1], axis=1)).astype(jnp.int32)
    send = jnp.stack([first, second], axis=1).reshape(-1)
    leaf_points = jnp.moveaxis(points.reshape(DIMS, LEAF_DEV, LEAF_PTS), 1, 0)
    got_points = lax.all_to_all(jnp.take(leaf_points, send, axis=0), "leaf", 0, 0, tiled=True)
    got_samples = lax.all_to_all(jnp.take(omega.reshape(LEAF_DEV, LEAF_PTS, columns), send, axis=0), "leaf", 0, 0, tiled=True)
    mine = lax.dynamic_index_in_dim(tree, me, 0, keepdims=False)
    smaller = jnp.any(jnp.logical_and((mine[:, None] >> 2) == (mine[None, :] >> 2), mine[None, :] < mine[:, None]), axis=1)
    arrival = ((mine >> 2) * SLOTS + smaller.astype(jnp.int32)).reshape(LEAF_DEV, NEAR)

    def one(member):
        slots = lax.dynamic_index_in_dim(arrival, member, 0, keepdims=False)
        far = jnp.moveaxis(jnp.take(got_points, slots, axis=0), 0, 1).reshape(DIMS, NEAR * LEAF_PTS)
        samples = jnp.take(got_samples, slots, axis=0).reshape(NEAR * LEAF_PTS, columns)
        own = lax.dynamic_index_in_dim(leaf_points, member, 0, keepdims=False)
        return jnp.dot(kernel_tile(own, far), samples, preferred_element_type=F32)

    return lax.map(one, jnp.arange(LEAF_DEV, dtype=jnp.int32))


def call(kernel, out_shape, in_specs, out_specs, **more):
    return pl.pallas_call(
        kernel,
        out_shape=out_shape,
        in_specs=in_specs,
        out_specs=out_specs,
        compiler_params=pltpu.CompilerParams(vmem_limit_bytes=VMEM_LIMIT),
        **more,
    )


def shards(points, omega, near_lists, leaf_order, pivots):
    columns = omega.shape[1]
    near = near_lists.T
    leaves = omega.reshape(LEAF_DEV, LEAF_PTS, columns)
    shape = jax.ShapeDtypeStruct
    block = shape((LEAF_PTS, columns), BF16)
    smem = pl.BlockSpec(memory_space=SMEM)
    anywhere = pl.BlockSpec(memory_space=pl.ANY)
    pack_shape = shape((SLOTS, PACK, columns), BF16)
    table, *packs = call(
        send_kernel, [shape((T_LEN,), jnp.int32)] + [pack_shape] * BESIDE, [smem, smem] + vm(4), [smem] + vm(BESIDE)
    )(near, leaf_order, near, leaf_order.reshape(-1, 128), points, leaves)

    total_shape = shape((LEAF_DEV, LEAF_PTS, columns), F32)
    coupling_shape = shape((LEAF_DEV * SKEL, LEAF_DEV * SKEL), BF16)

    def shift(value, k):
        return lax.ppermute(value, "samp", [(s, (s + k) % 4) for s in range(4)])

    def turned(values):
        moved = {}
        for k in range(1, 4):
            moved[k] = shift(values[k], k)
        return [moved[k] for k in range(1, 4)]

    def near_branch(points, leaves, near_lists, leaf_order, pivots, table, packs):
        def move(pack, offset):
            return lax.ppermute(pack, "leaf", [((n + offset[n % 2]) % NODES, n) for n in range(NODES)])

        arrived = []
        for i in range(BESIDE):
            arrived.append(move(packs[i], OFFSETS[i]))
        total, left = call(
            own_kernel, [total_shape, shape((LEAF_DEV * LEAF_PTS, AUG), BF16)], [smem] + vm(2), vm(2)
        )(table, points, leaves)
        skeleton, beside, half = call(
            half_kernel,
            [shape((DIMS, LEAF_DEV * SKEL), BF16), shape((SLOTS, PACK + SLOTS * DIMS, columns), BF16), pack_shape],
            [smem] + vm(3) + [anywhere] * 2,
            vm(3),
        )(table, points, leaves, pivots, left, arrived[0])
        arrived.append(move(beside, OFFSETS[BESIDE]))
        arrived.append(move(half, OFFSETS[HALF]))
        first, second, last = GROUPS
        (total,) = call(
            functools.partial(early_kernel, first), [total_shape], [smem] + vm(2 + len(first)), vm(1)
        )(table, left, total, *[arrived[i] for i in first])
        total, coupling = call(
            functools.partial(couple_kernel, second), [total_shape, coupling_shape], [smem] + vm(4 + len(second)), vm(2)
        )(table, left, total, skeleton, arrived[BESIDE], *[arrived[i] for i in second])
        total, *blocks = call(
            functools.partial(late_kernel, last), [total_shape] + [block] * 4, [smem] + vm(2 + len(last)), vm(5)
        )(table, left, total, *[arrived[i] for i in last])
        return total, blocks, coupling

    def any_branch(points, leaves, near_lists, leaf_order, pivots, table, packs):
        total = general_sample(points, leaves.reshape(-1, columns), near_lists, leaf_order)
        column = lax.axis_index("samp")
        blocks = [lax.dynamic_index_in_dim(total, (column + k) & 3, 0, keepdims=False).astype(BF16) for k in range(4)]
        skeleton = jnp.take_along_axis(points.reshape(DIMS, LEAF_DEV, LEAF_PTS), pivots[None], axis=2)
        skeleton = skeleton.reshape(DIMS, LEAF_DEV * SKEL)
        return total, blocks, kernel_tile(skeleton, lax.ppermute(skeleton, "leaf", [(n, n ^ 1) for n in range(NODES)]))

    total, blocks, coupling = lax.cond(
        table[T_OK] > 0, near_branch, any_branch, points, leaves, near_lists, leaf_order, pivots, table, packs
    )
    swapped = [blocks[0]] + turned(blocks)
    (rows,) = call(rows_kernel, [shape((LEAF_DEV * SKEL, columns), F32)], vm(2), vm(1))(total, pivots)
    (interpolation,) = call(
        solve_kernel, [shape((LEAF_PTS, SKEL), BF16)], vm(5) + [anywhere], vm(1)
    )(*swapped, pivots, rows)
    spread = [interpolation] + turned([interpolation] * 4)
    projected_shape = [shape((LEAF_DEV * SKEL, columns), BF16)]
    (projected,) = call(functools.partial(project_kernel, FIRST), projected_shape, vm(1 + len(FIRST)), vm(1))(
        leaves, *[spread[k] for k in FIRST]
    )
    (projected,) = call(functools.partial(project_kernel, SECOND), projected_shape, vm(2 + len(SECOND)), vm(1))(
        leaves, projected, *[spread[k] for k in SECOND]
    )
    crossed = lax.ppermute(projected, "leaf", [(n, n ^ 1) for n in range(NODES)])
    (stacked,) = call(stack_kernel, [shape((LEAF_DEV * LEAF_PTS, SKEL), BF16)], vm(4), vm(1))(*spread)
    (parent,) = call(parent_kernel, [shape((LEAF_DEV * SKEL, columns), F32)], vm(3), vm(1))(rows, coupling, crossed)
    return stacked, parent


def solution(mesh):
    placed = (P(None, "leaf"), P("leaf", "samp"), P(), P(), P("leaf", None))
    return jax.shard_map(
        shards,
        mesh=mesh,
        in_specs=placed,
        out_specs=(P("leaf", None), P("leaf", "samp")),
        check_vma=False,
    )
```

```python
import functools

import jax
import jax.numpy as jnp
from jax import lax
from jax.experimental import pallas as pl
from jax.experimental.pallas import tpu as pltpu
from jax.sharding import PartitionSpec as P


DIMS = 8
LEAF_PTS = 512
NEAR = 8
SKEL = 128
SLOTS = 2
LEAF_DEV = 4
REACH = 3
LEAVES = 256
NODES = LEAVES // LEAF_DEV
RIDGE = 0.1
RATE = 0.25

AUG = 16
PACK = LEAF_PTS + DIMS * LEAF_PTS // 128
SIBLING, BEHIND, BEHIND_ACROSS, AHEAD, MIXED, FAR = (1, -1), (-2, -2), (-1, -3), (2, 2), (-3, 1), (NODES // 2, NODES // 2)
OFFSETS = (BEHIND, BEHIND_ACROSS, AHEAD, MIXED, SIBLING, FAR)
CLASSES = len(OFFSETS)
HALF = CLASSES - 1
BESIDE = CLASSES - 2
GROUPS = ((4, 0, 1), (2, 3), (HALF,))
FIRST, SECOND = (0,), (1, 2, 3)
T_LEAF = 96
T_OK = 0
T_OWN = 8
T_FAR = 32
T_LEN = 128
VMEM_LIMIT = 16 << 20

VMEM = pltpu.VMEM
SMEM = pltpu.SMEM
F32 = jnp.float32
BF16 = jnp.bfloat16
HIGHEST = lax.Precision.HIGHEST


def vm(count):
    return [pl.BlockSpec(memory_space=VMEM)] * count


def dot_tn(a, b):
    return lax.dot_general(a, b, (((0,), (0,)), ((), ())), preferred_element_type=F32)


def dot_nt(a, b):
    return lax.dot_general(a, b, (((1,), (1,)), ((), ())), preferred_element_type=F32)


def split_norm(coords):
    norm = RATE * jnp.sum(coords * coords, axis=0, keepdims=True)
    high = norm.astype(BF16).astype(F32)
    rest = norm - high
    middle = rest.astype(BF16).astype(F32)
    low = rest - middle
    return high, middle, low


def left_side(coords):
    high, middle, low = split_norm(coords)
    row = lax.broadcasted_iota(jnp.int32, (DIMS, coords.shape[1]), 0)
    extra = jnp.where(row == 0, -high, jnp.where(row == 1, -middle, jnp.where(row == 2, -low, jnp.where(row < 6, 1.0, 0.0))))
    return jnp.concatenate([coords * (2.0 * RATE), extra], axis=0).astype(BF16)


def right_side(coords):
    high, middle, low = split_norm(coords)
    row = lax.broadcasted_iota(jnp.int32, (DIMS, coords.shape[1]), 0)
    extra = jnp.where(row == 3, -high, jnp.where(row == 4, -middle, jnp.where(row == 5, -low, jnp.where(row < 3, 1.0, 0.0))))
    return jnp.concatenate([coords, extra], axis=0).astype(BF16)


def fill_pack(pack, leaves, points, omega):
    for slot, leaf in enumerate(leaves):
        pack[slot, 0:LEAF_PTS, :] = omega[leaf]
        mine = points[:, pl.ds(pl.multiple_of(leaf * LEAF_PTS, LEAF_PTS), LEAF_PTS)]
        for piece in range(LEAF_PTS // 128):
            pack[slot, LEAF_PTS + DIMS * piece:LEAF_PTS + DIMS * (piece + 1), :] = mine[:, 128 * piece:128 * (piece + 1)]


def send_kernel(near_s, order_s, near_v, order_v, points, omega, table, *packs):
    me = lax.axis_index("leaf")
    halves = [jnp.broadcast_to(order_v[part:part + 1, :], (NEAR, 128)) for part in range(LEAVES // 128)]

    def look(near):
        found = jnp.zeros((NEAR, 128), jnp.int32)
        for part, half in enumerate(halves):
            here = jnp.take_along_axis(half, near & 127, axis=1, mode="promise_in_bounds")
            found = jnp.where(near >> 7 == part, here, found)
        return found

    near = near_v[...]
    tree = jnp.concatenate([look(near[:, 128 * part:128 * (part + 1)]) for part in range(LEAVES // 128)], axis=1)
    node = lax.broadcasted_iota(jnp.int32, (NEAR, LEAVES), 1) >> 2
    part = tree & 3
    weight = jnp.where(part == 0, 1.0, jnp.where(part == 1, 8.0, jnp.where(part == 2, 64.0, 512.0)))
    weight = jnp.where((tree >> 2) == me, weight, 0.0)
    for index, offset in enumerate(OFFSETS):
        even, odd = offset
        requester = (me - jnp.where((me ^ even) & 1 > 0, odd, even)) & (NODES - 1)
        counts = jnp.sum(jnp.where(node == requester, weight, 0.0)).astype(jnp.int32)
        has = [(counts >> (3 * leaf)) & 7 > 0 for leaf in range(LEAF_DEV)]
        first = jnp.where(has[0], 0, jnp.where(has[1], 1, jnp.where(has[2], 2, jnp.where(has[3], 3, 0))))
        second = jnp.where(has[3], 3, jnp.where(has[2], 2, jnp.where(has[1], 1, 0)))
        if index >= BESIDE:
            table[T_LEAF + 2 * index], table[T_LEAF + 2 * index + 1] = first, second
        else:
            fill_pack(packs[index], (first, second), points, omega)

    place = ((tree >> 2) - node + REACH) & (NODES - 1)
    bad = jnp.logical_and(place >= 2 * REACH, place != REACH + NODES // 2)
    table[T_OK] = jnp.where(jnp.max(jnp.where(bad, 1.0, 0.0)) > 0.0, 0, 1)

    def lowest(mask):
        return jnp.where(mask & 1 > 0, 0, jnp.where(mask & 2 > 0, 1, jnp.where(mask & 4 > 0, 2, jnp.where(mask & 8 > 0, 3, 0))))

    def highest(mask):
        return jnp.where(mask & 8 > 0, 3, jnp.where(mask & 4 > 0, 2, jnp.where(mask & 2 > 0, 1, 0)))

    masks = []
    for member in range(LEAF_DEV):
        mask = jnp.int32(0)
        for entry in range(NEAR):
            leaf = order_s[near_s[entry, me * LEAF_DEV + member]]
            spot = ((leaf >> 2) - me + REACH) & (NODES - 1)
            spot = jnp.where(spot < 2 * REACH, spot, 2 * REACH)
            mask = mask | (jnp.int32(1) << (4 * spot + (leaf & 3)))
        masks.append(mask)
    every = masks[0] | masks[1] | masks[2] | masks[3]
    for member in range(LEAF_DEV):
        for source in range(LEAF_DEV):
            table[T_OWN + LEAF_DEV * member + source] = (masks[member] >> (4 * REACH + source)) & 1
    for index, offset in enumerate(OFFSETS):
        spot = 2 * REACH if index == HALF else jnp.where(me & 1 > 0, offset[1], offset[0]) + REACH
        four = (every >> (4 * spot)) & 15
        first, second = lowest(four), highest(four)
        for member in range(LEAF_DEV):
            bits = masks[member] >> (4 * spot)
            table[T_FAR + 8 * index + 2 * member] = (bits >> first) & 1
            table[T_FAR + 8 * index + 2 * member + 1] = jnp.where(first == second, 0, (bits >> second) & 1)


def add_tile(left, right, samples, total, member):
    start = pl.multiple_of(member * LEAF_PTS, LEAF_PTS)
    exponent = jnp.dot(left[pl.ds(start, LEAF_PTS), :], right, preferred_element_type=F32)
    tile = jnp.exp(exponent).astype(BF16)
    total[member] += jnp.dot(tile, samples, preferred_element_type=F32)


def own_kernel(table, points, omega, total, left):
    for member in range(LEAF_DEV):
        coords = points[:, member * LEAF_PTS:(member + 1) * LEAF_PTS]
        left[member * LEAF_PTS:(member + 1) * LEAF_PTS, :] = left_side(coords.astype(F32)).astype(F32).T.astype(BF16)
    total[...] = jnp.zeros_like(total)

    def source_step(source, carry):
        coords = points[:, pl.ds(pl.multiple_of(source * LEAF_PTS, LEAF_PTS), LEAF_PTS)]
        right = right_side(coords.astype(F32))
        samples = omega[source]

        def member_step(member, inner):
            @pl.when(table[T_OWN + LEAF_DEV * member + source] > 0)
            def _():
                add_tile(left, right, samples, total, member)

            return inner

        return lax.fori_loop(0, LEAF_DEV, member_step, carry)

    lax.fori_loop(0, LEAF_DEV, source_step, 0)


def half_kernel(table, points, omega, pivots, left, behind, skeleton, beside, half):
    del left, behind
    for index, pack in ((BESIDE, beside), (HALF, half)):
        fill_pack(pack, (table[T_LEAF + 2 * index], table[T_LEAF + 2 * index + 1]), points, omega)
    for member in range(LEAF_DEV):
        coords = points[:, member * LEAF_PTS:(member + 1) * LEAF_PTS]
        chosen = lax.broadcasted_iota(jnp.int32, (LEAF_PTS, SKEL), 0) == pivots[member:member + 1, :]
        picked = jnp.dot(coords, jnp.where(chosen, 1.0, 0.0).astype(BF16), preferred_element_type=F32).astype(BF16)
        skeleton[:, member * SKEL:(member + 1) * SKEL] = picked
        slot, row = divmod(member, SLOTS)
        beside[slot, PACK + DIMS * row:PACK + DIMS * (row + 1), :] = picked


def add_packs(group, table, left, packs, total):
    for index, pack in zip(group, packs):

        def slot_step(slot, carry, index=index, pack=pack):
            pieces = [pack[slot, LEAF_PTS + DIMS * c:LEAF_PTS + DIMS * (c + 1), :] for c in range(LEAF_PTS // 128)]
            coords = jnp.concatenate([p.astype(F32) for p in pieces], axis=1)
            right = right_side(coords)
            samples = pack[slot, 0:LEAF_PTS, :]

            def member_step(member, inner):
                @pl.when(table[T_FAR + 8 * index + 2 * member + slot] > 0)
                def _():
                    add_tile(left, right, samples, total, member)

                return inner

            return lax.fori_loop(0, LEAF_DEV, member_step, carry)

        lax.fori_loop(0, SLOTS, slot_step, 0)


def early_kernel(group, table, left, before, *rest):
    packs, (total,) = rest[:len(group)], rest[len(group):]
    total[...] = before[...]
    add_packs(group, table, left, packs, total)


def couple_kernel(group, table, left, before, skeleton, beside, *rest):
    packs, (total, coupling) = rest[:len(group)], rest[len(group):]
    early_kernel(group, table, left, before, *packs, total)
    places = [divmod(member, SLOTS) for member in range(LEAF_DEV)]
    pieces = [beside[slot, PACK + DIMS * row:PACK + DIMS * (row + 1), :] for slot, row in places]
    sibling = jnp.concatenate([piece.astype(F32) for piece in pieces], axis=1)
    exponent = dot_tn(left_side(skeleton[...].astype(F32)), right_side(sibling))
    coupling[...] = jnp.exp(exponent).astype(BF16)


def late_kernel(group, table, left, before, *rest):
    packs, (low, *blocks, total) = rest[:len(group)], rest[len(group):]
    total[...] = before[...]
    add_packs(group, table, left, packs, total)
    column = lax.axis_index("samp")
    for step in range(4):
        values = total[(column + step) & 3]
        high = values.astype(BF16)
        blocks[step][...] = high
        low[step] = (values - high.astype(F32)).astype(BF16)


def rows_kernel(low, b0, b1, b2, b3, pivots, rows):
    column = lax.axis_index("samp")
    for step, block in enumerate((b0, b1, b2, b3)):
        member = (column + step) & 3
        chosen = lax.broadcasted_iota(jnp.int32, (LEAF_PTS, SKEL), 0) == pivots[pl.ds(member, 1), :]
        pick = jnp.where(chosen, 1.0, 0.0).astype(BF16)
        spot = pl.ds(pl.multiple_of(member * SKEL, SKEL), SKEL)
        rows[spot, :] = dot_tn(pick, block[...]) + dot_tn(pick, low[step])


def matmul3(a, b):
    a_high = a.astype(BF16)
    a_low = (a - a_high.astype(F32)).astype(BF16)
    b_high = b.astype(BF16)
    b_low = (b - b_high.astype(F32)).astype(BF16)
    left = jnp.concatenate([a_high, a_high, a_low], axis=1)
    right = jnp.concatenate([b_high, b_low, b_high], axis=0)
    return jnp.dot(left, right, preferred_element_type=F32)


def inverse(gram):
    row = lax.broadcasted_iota(jnp.int32, (SKEL, SKEL), 0)
    eye = jnp.where(row == lax.broadcasted_iota(jnp.int32, (SKEL, SKEL), 1), 1.0, 0.0)
    trace = jnp.sum(jnp.sum(gram * eye, axis=1, keepdims=True), axis=0, keepdims=True)
    shift = RIDGE * trace / SKEL
    scaled = gram / shift + eye
    spread = 1.0 + SKEL / RIDGE
    error = (spread - 1.0) / (spread + 1.0)
    start = 2.0 / (1.0 + spread)
    guess = start * (2.0 * eye - start * scaled)
    error = error * error
    while error > 1e-5:
        factor = 2.0 / (2.0 - error)
        guess = guess * factor
        error = error / (2.0 - error)
        late = error < 0.1
        multiply = functools.partial(jnp.dot, precision=HIGHEST, preferred_element_type=F32) if late else matmul3
        guess = 2.0 * guess - multiply(guess, multiply(scaled, guess))
        error = error * error
    return guess / shift


def solve_kernel(b0, b1, b2, b3, pivots, rows, interpolation):
    del rows
    column = lax.axis_index("samp")
    mine = pivots[pl.ds(column, 1), :]
    chosen = lax.broadcasted_iota(jnp.int32, (LEAF_PTS, SKEL), 0) == mine
    pick = jnp.where(chosen, 1.0, 0.0).astype(BF16)
    gram = jnp.zeros((SKEL, SKEL), F32)
    cross = jnp.zeros((LEAF_PTS, SKEL), F32)
    for block in (b0, b1, b2, b3):
        values = block[...]
        rows = dot_tn(pick, values).astype(BF16)
        gram += dot_nt(rows, rows)
        cross += dot_nt(values, rows)
    interpolation[...] = jnp.dot(cross, inverse(gram), precision=HIGHEST, preferred_element_type=F32).astype(BF16)


def project_kernel(steps, omega, *rest):
    column = lax.axis_index("samp")
    projected = rest[-1]
    if len(rest) > len(steps) + 1:
        projected[...] = rest[0][...]
    for step, block in zip(steps, rest[-1 - len(steps):-1]):
        leaf = (column - step) & 3
        spot = pl.ds(pl.multiple_of(leaf * SKEL, SKEL), SKEL)
        projected[spot, :] = dot_tn(block[...], omega[leaf]).astype(BF16)


def stack_kernel(i0, i1, i2, i3, interpolation):
    column = lax.axis_index("samp")
    for step, block in enumerate((i0, i1, i2, i3)):
        leaf = (column - step) & 3
        interpolation[pl.ds(pl.multiple_of(leaf * LEAF_PTS, LEAF_PTS), LEAF_PTS), :] = block[...]


def parent_kernel(rows, coupling, projected, parent):
    parent[...] = rows[...] - jnp.dot(coupling[...], projected[...], preferred_element_type=F32)


def kernel_tile(own, far):
    own_f, far_f = own.astype(F32), far.astype(F32)
    inner = jnp.dot(own.T, far, preferred_element_type=F32)
    distance = jnp.sum(own_f * own_f, 0)[:, None] + jnp.sum(far_f * far_f, 0)[None, :] - 2.0 * inner
    return jnp.exp(-RATE * distance).astype(BF16)


def general_sample(points, omega, near_lists, leaf_order):
    nodes = lax.axis_size("leaf")
    me = lax.axis_index("leaf")
    columns = omega.shape[1]
    references = LEAF_DEV * NEAR
    tree = jnp.take(leaf_order, near_lists, axis=0).reshape(nodes, references)
    leaf = lax.broadcasted_iota(jnp.int32, (1, 1, LEAF_DEV), 2)
    wants = jnp.any(tree[:, :, None] == me * LEAF_DEV + leaf, axis=1)
    first = jnp.argmax(wants, axis=1).astype(jnp.int32)
    second = (LEAF_DEV - 1 - jnp.argmax(wants[:, ::-1], axis=1)).astype(jnp.int32)
    send = jnp.stack([first, second], axis=1).reshape(-1)
    leaf_points = jnp.moveaxis(points.reshape(DIMS, LEAF_DEV, LEAF_PTS), 1, 0)
    got_points = lax.all_to_all(jnp.take(leaf_points, send, axis=0), "leaf", 0, 0, tiled=True)
    got_samples = lax.all_to_all(jnp.take(omega.reshape(LEAF_DEV, LEAF_PTS, columns), send, axis=0), "leaf", 0, 0, tiled=True)
    mine = lax.dynamic_index_in_dim(tree, me, 0, keepdims=False)
    smaller = jnp.any(jnp.logical_and((mine[:, None] >> 2) == (mine[None, :] >> 2), mine[None, :] < mine[:, None]), axis=1)
    arrival = ((mine >> 2) * SLOTS + smaller.astype(jnp.int32)).reshape(LEAF_DEV, NEAR)

    def one(member):
        slots = lax.dynamic_index_in_dim(arrival, member, 0, keepdims=False)
        far = jnp.moveaxis(jnp.take(got_points, slots, axis=0), 0, 1).reshape(DIMS, NEAR * LEAF_PTS)
        samples = jnp.take(got_samples, slots, axis=0).reshape(NEAR * LEAF_PTS, columns)
        own = lax.dynamic_index_in_dim(leaf_points, member, 0, keepdims=False)
        return jnp.dot(kernel_tile(own, far), samples, preferred_element_type=F32)

    return lax.map(one, jnp.arange(LEAF_DEV, dtype=jnp.int32))


def call(kernel, out_shape, in_specs, out_specs, **more):
    return pl.pallas_call(
        kernel,
        out_shape=out_shape,
        in_specs=in_specs,
        out_specs=out_specs,
        compiler_params=pltpu.CompilerParams(vmem_limit_bytes=VMEM_LIMIT),
        **more,
    )


def shards(points, omega, near_lists, leaf_order, pivots):
    columns = omega.shape[1]
    near = near_lists.T
    leaves = omega.reshape(LEAF_DEV, LEAF_PTS, columns)
    shape = jax.ShapeDtypeStruct
    block = shape((LEAF_PTS, columns), BF16)
    smem = pl.BlockSpec(memory_space=SMEM)
    anywhere = pl.BlockSpec(memory_space=pl.ANY)
    pack_shape = shape((SLOTS, PACK, columns), BF16)
    table, *packs = call(
        send_kernel, [shape((T_LEN,), jnp.int32)] + [pack_shape] * BESIDE, [smem, smem] + vm(4), [smem] + vm(BESIDE)
    )(near, leaf_order, near, leaf_order.reshape(-1, 128), points, leaves)

    total_shape = shape((LEAF_DEV, LEAF_PTS, columns), F32)
    low_shape = shape((LEAF_DEV, LEAF_PTS, columns), BF16)
    coupling_shape = shape((LEAF_DEV * SKEL, LEAF_DEV * SKEL), BF16)

    def shift(value, k):
        return lax.ppermute(value, "samp", [(s, (s + k) % 4) for s in range(4)])

    def turned(values):
        moved = {}
        for k in range(1, 4):
            moved[k] = shift(values[k], k)
        return [moved[k] for k in range(1, 4)]

    def near_branch(points, leaves, near_lists, leaf_order, pivots, table, packs):
        def move(pack, offset):
            return lax.ppermute(pack, "leaf", [((n + offset[n % 2]) % NODES, n) for n in range(NODES)])

        arrived = []
        for i in range(BESIDE):
            arrived.append(move(packs[i], OFFSETS[i]))
        total, left = call(
            own_kernel, [total_shape, shape((LEAF_DEV * LEAF_PTS, AUG), BF16)], [smem] + vm(2), vm(2)
        )(table, points, leaves)
        skeleton, beside, half = call(
            half_kernel,
            [shape((DIMS, LEAF_DEV * SKEL), BF16), shape((SLOTS, PACK + SLOTS * DIMS, columns), BF16), pack_shape],
            [smem] + vm(3) + [anywhere] * 2,
            vm(3),
        )(table, points, leaves, pivots, left, arrived[0])
        arrived.append(move(beside, OFFSETS[BESIDE]))
        arrived.append(move(half, OFFSETS[HALF]))
        first, second, last = GROUPS
        (total,) = call(
            functools.partial(early_kernel, first), [total_shape], [smem] + vm(2 + len(first)), vm(1)
        )(table, left, total, *[arrived[i] for i in first])
        total, coupling = call(
            functools.partial(couple_kernel, second), [total_shape, coupling_shape], [smem] + vm(4 + len(second)), vm(2)
        )(table, left, total, skeleton, arrived[BESIDE], *[arrived[i] for i in second])
        low, *blocks = call(
            functools.partial(late_kernel, last),
            [low_shape] + [block] * 4,
            [smem] + vm(2 + len(last)),
            vm(5),
            scratch_shapes=[pltpu.VMEM(total_shape.shape, F32)],
        )(table, left, total, *[arrived[i] for i in last])
        return low, blocks, coupling

    def any_branch(points, leaves, near_lists, leaf_order, pivots, table, packs):
        total = general_sample(points, leaves.reshape(-1, columns), near_lists, leaf_order)
        column = lax.axis_index("samp")
        turned_total = [lax.dynamic_index_in_dim(total, (column + k) & 3, 0, keepdims=False) for k in range(4)]
        blocks = [value.astype(BF16) for value in turned_total]
        low = jnp.stack([(v - h.astype(F32)).astype(BF16) for v, h in zip(turned_total, blocks)])
        skeleton = jnp.take_along_axis(points.reshape(DIMS, LEAF_DEV, LEAF_PTS), pivots[None], axis=2)
        skeleton = skeleton.reshape(DIMS, LEAF_DEV * SKEL)
        return low, blocks, kernel_tile(skeleton, lax.ppermute(skeleton, "leaf", [(n, n ^ 1) for n in range(NODES)]))

    low, blocks, coupling = lax.cond(
        table[T_OK] > 0, near_branch, any_branch, points, leaves, near_lists, leaf_order, pivots, table, packs
    )
    swapped = [blocks[0]] + turned(blocks)
    (rows,) = call(rows_kernel, [shape((LEAF_DEV * SKEL, columns), F32)], vm(6), vm(1))(low, *blocks, pivots)
    (interpolation,) = call(
        solve_kernel, [shape((LEAF_PTS, SKEL), BF16)], vm(5) + [anywhere], vm(1)
    )(*swapped, pivots, rows)
    spread = [interpolation] + turned([interpolation] * 4)
    projected_shape = [shape((LEAF_DEV * SKEL, columns), BF16)]
    (projected,) = call(functools.partial(project_kernel, FIRST), projected_shape, vm(1 + len(FIRST)), vm(1))(
        leaves, *[spread[k] for k in FIRST]
    )
    (projected,) = call(functools.partial(project_kernel, SECOND), projected_shape, vm(2 + len(SECOND)), vm(1))(
        leaves, projected, *[spread[k] for k in SECOND]
    )
    crossed = lax.ppermute(projected, "leaf", [(n, n ^ 1) for n in range(NODES)])
    (stacked,) = call(stack_kernel, [shape((LEAF_DEV * LEAF_PTS, SKEL), BF16)], vm(4), vm(1))(*spread)
    (parent,) = call(parent_kernel, [shape((LEAF_DEV * SKEL, columns), F32)], vm(3), vm(1))(rows, coupling, crossed)
    return stacked, parent


def solution(mesh):
    placed = (P(None, "leaf"), P("leaf", "samp"), P(), P(), P("leaf", None))
    return jax.shard_map(
        shards,
        mesh=mesh,
        in_specs=placed,
        out_specs=(P("leaf", None), P("leaf", "samp")),
        check_vma=False,
    )
```
